512 devices in a mesh: elem: 128 (over y, z, core), lev: 4 (over x).
Axes of the slice: x: 4, y: 8, z: 8, core: 2. Of those that a mesh axis runs over, the one named last changes fastest.
Arguments:
- fields: float32 [10, 128, 131072], P(None, 'lev', 'elem'), may hold values from -6 to 6
- coupling: float32 [128, 131072], P('lev', 'elem'), may hold values from 5 to 3000
- column_map: int32 [131072], P('elem'), may hold values from 0 to 1023, as said below
- sunlit: int32 [1024], P(('elem', 'lev')), may hold values from 0 to 1, as said below
- cloudy: int32 [131072], P(('elem', 'lev')), may hold values 0 or 1
- radiation_in: bfloat16 [256, 256], replicated, may hold values from -0.375 to 0.375
- radiation_out: bfloat16 [256, 128], replicated, may hold values from -0.375 to 0.375
Outputs:
- tendency: bfloat16 [10, 128, 131072], P(None, 'lev', 'elem')
The draws below stay inside these ranges and needn't reach their ends.
Inputs may be any that keep to these rules, and one draw needn't show every extreme that they name: `column_map`: every run of 1024 entries starting at a multiple of 1024 is a permutation of 0 to 1023. For every block b below 512, exactly one of blocks b and b + 512 is sunlit.
All inputs are finite; a program needn't handle non-finite values. No bound on the sum of `cloudy` on one device may be relied on, other than what follows from the above.
Results may differ from the reference program's by a relative error of at most 0.001.
Values may be sent and summed in bfloat16 or wider, within the bound.
A program may use at most 128 MiB of HBM per device.

```python
import math
import jax
import jax.numpy as jnp
from jax import lax

F = 10
L = 128
HID = 256
BLK = 128
COL_DEV = 1024
NCOL = 131072
NBT = 1024
N_ELEM = 128
N_LEV = 4


def draw_column_map(key, part):
    tiles = NCOL // COL_DEV
    keys = jax.random.split(jax.random.fold_in(key, 11), tiles)
    orders = jax.vmap(lambda single: jax.random.permutation(single, COL_DEV))(keys)
    return orders.reshape(NCOL).astype(jnp.int32)


def draw_sunlit(key, part):
    start = jax.random.randint(jax.random.fold_in(key, 23), (), 0, NBT)
    position = (jnp.arange(NBT, dtype=jnp.int32) - start) % NBT
    return (position < NBT // 2).astype(jnp.int32)


def place_ends(values, own_key, low, top_value):
    shape = values.shape
    spot = [jax.random.randint(jax.random.fold_in(own_key, axis), (), 0, shape[axis]) for axis in range(len(shape))]
    values = values.at[tuple(spot)].set(low)
    longest = shape.index(max(shape))
    spot[longest] = (spot[longest] + 1) % shape[longest]
    return values.at[tuple(spot)].set(top_value)


def level_of(key, extent, cuts, least, top_value):
    loudness = 1.0
    for dim, parts in cuts:
        heights = jax.random.uniform(jax.random.fold_in(jax.random.fold_in(key, 6), dim), (parts,), jnp.float32, least / len(cuts), top_value / len(cuts))
        loudness = loudness * jnp.repeat(jnp.exp(heights), extent[dim] // parts).reshape((-1,) + (1,) * (len(extent) - 1 - dim))
    return loudness


def noise(own_key, shape, width, limit, cuts=(), kind=jnp.bfloat16):
    values = width * jax.random.normal(own_key, shape, jnp.float32)
    if cuts:
        values = values * level_of(own_key, shape, cuts, -0.22, 0.18)
    return jnp.clip(values, -limit, limit).astype(kind)


def setup_inputs(seed: int = 0) -> dict:
    key_list = jax.random.split(jax.random.key(seed), 8)
    fields = noise(key_list[0], (F, L, NCOL), 1.0, 6.0, ((1, 4), (2, 128)), jnp.float32)
    coupling = jnp.clip(jnp.exp(math.log(3000.0) - 6.3969297 * jax.random.uniform(key_list[1], (L, NCOL), jnp.float32) ** level_of(key_list[1], (L, NCOL), ((0, 4), (1, 128)), -0.2, 0.2)), 5.0, 3000.0)
    column_map = draw_column_map(jax.random.fold_in(key_list[7], 71), 0)
    sunlit = draw_sunlit(jax.random.fold_in(key_list[7], 71), 0)
    cloudy = place_ends((jax.random.randint(key_list[4], (NCOL,), 0, 3) < 1).astype(jnp.int32), jax.random.fold_in(key_list[4], 1), 0, 1)
    radiation_in = noise(key_list[5], (2 * L, HID), (2 * L) ** -0.5, 0.375)
    radiation_out = noise(key_list[6], (HID, L), HID ** -0.5, 0.375)
    return dict(fields=fields, coupling=coupling, column_map=column_map, sunlit=sunlit, cloudy=cloudy, radiation_in=radiation_in, radiation_out=radiation_out)


NU_HYPER = 0.05
CLOUD_SHADE = 0.6

def hyper_term(fields):
    second = jnp.roll(fields, 1, axis=2) - 2.0 * fields + jnp.roll(fields, -1, axis=2)
    fourth = jnp.roll(second, 1, axis=2) - 2.0 * second + jnp.roll(second, -1, axis=2)
    return -NU_HYPER * fourth

def group_source(column_map):
    per_peer = COL_DEV // N_ELEM
    quarter = per_peer // N_LEV
    group_cols = COL_DEV // N_LEV
    position = jnp.arange(NCOL, dtype=jnp.int32)
    owner = position // COL_DEV
    within = position % COL_DEV
    lev_part = within // group_cols
    offset = within % group_cols
    anchor = offset // quarter
    inner = offset % quarter
    slot = owner * per_peer + lev_part * quarter + inner
    return anchor * COL_DEV + jnp.take(column_map, anchor * COL_DEV + slot)

def reference(fields, coupling, column_map, sunlit, cloudy, radiation_in, radiation_out):
    source = group_source(column_map)
    group_cols = COL_DEV // N_LEV
    pieces = NCOL // group_cols

    def piece(index):
        cols = lax.dynamic_slice_in_dim(source, index * group_cols, group_cols)
        group = jnp.take(fields, cols, axis=2)
        group_coupling = jnp.take(coupling, cols, axis=1)
        sun_blocks = lax.dynamic_slice_in_dim(sunlit, index * (group_cols // BLK), group_cols // BLK)
        cloud_cols = lax.dynamic_slice_in_dim(cloudy, index * group_cols, group_cols)
        rad_input = group[:2].reshape(2 * L, group_cols).astype(jnp.bfloat16)
        rad_hidden = jnp.tanh(jnp.dot(radiation_in.T.astype(jnp.float32), rad_input.astype(jnp.float32), preferred_element_type=jnp.float32)).astype(jnp.bfloat16)
        heating = jnp.dot(radiation_out.T.astype(jnp.float32), rad_hidden.astype(jnp.float32), preferred_element_type=jnp.float32)
        factor = jnp.repeat(sun_blocks, BLK) * (1.0 - CLOUD_SHADE * cloud_cols)
        heating = heating * factor[None, :]
        forced = group.at[0].add(heating)
        zero_row = jnp.zeros((1, group_cols), jnp.float32)
        sub_diag = jnp.concatenate([zero_row, -group_coupling[:-1]], axis=0)
        super_diag = jnp.concatenate([-group_coupling[:-1], zero_row], axis=0)
        main_diag = 1.0 - sub_diag - super_diag
        solved = lax.linalg.tridiagonal_solve(sub_diag.T, main_diag.T, super_diag.T, forced.transpose(2, 1, 0))
        return solved.transpose(2, 1, 0) - group
    increments = lax.map(piece, jnp.arange(pieces, dtype=jnp.int32))
    increment = increments.transpose(1, 2, 0, 3).reshape(F, L, NCOL)
    placed = jnp.zeros_like(fields).at[:, :, source].set(increment)
    return (placed + hyper_term(fields)).astype(jnp.bfloat16)
```

```python
import functools

import jax
import jax.numpy as jnp
from jax import lax
from jax.experimental import pallas as pl
from jax.experimental.pallas import tpu as pltpu
from jax.sharding import PartitionSpec as P

NU_HYPER = 0.05
CLOUD_SHADE = 0.6
MESH = pl.DeviceIdType.MESH

F = 10
NL = 4
NY = 8
NZC = 16
NE = NY * NZC
LB = 32
COLS = 1024
C = COLS // 128
ROWS = F * LB


def dot0(a, b):
    return lax.dot_general(a, b, (((0,), (0,)), ((), ())), preferred_element_type=jnp.float32)


def dot1(a, b):
    return lax.dot_general(a, b, (((1,), (1,)), ((), ())), preferred_element_type=jnp.float32)


def kernel(
    f_hbm, k_hbm, cm_hbm, sun_ref, cl_hbm, wi_hbm, wo_hbm, out_hbm,
    fb, kb, cm, cl, wi, wo, rb, hs, hr, sb, yb, ys, zb, xr, onehot,
    gb, rk, rt, ub, vb, ifb, hib, hb, hy, xb, nb, ob,
    load_sem, out_sem, y_s, y_r, z_s, z_r, x_s, x_r, rad_s, rad_r, halo_s, halo_r, if_s, if_r, hi_s, hi_r,
):
    e = lax.axis_index("elem")
    l = lax.axis_index("lev")
    y, zc = e // NZC, e % NZC

    def lev_peer(d):
        return (e, (l + d) % NL)

    def y_peer(d):
        return (((y + d) % NY) * NZC + zc, l)

    def z_peer(d):
        return (y * NZC + (zc + d) % NZC, l)

    right, left = ((e + 1) % NE, l), ((e + NE - 1) % NE, l)

    barrier = pltpu.get_barrier_semaphore()
    peers = [y_peer(d) for d in range(1, NY)] + [z_peer(d) for d in range(1, NZC)]
    peers += [lev_peer(d) for d in range(1, NL)] + [right, left]
    for peer in peers:
        pl.semaphore_signal(barrier, inc=1, device_id=peer, device_id_type=MESH)

    loads = []

    def load(src, dst):
        copy = pltpu.make_async_copy(src, dst, load_sem.at[len(loads)])
        copy.start()
        loads.append(copy)
        return copy

    head = [load(f_hbm.at[pl.ds(0, 64), pl.ds(c * 128, 128)], fb.at[pl.ds(c * ROWS, 64), :]) for c in range(C)]
    small = [load(cl_hbm, cl), load(cm_hbm, cm), load(wo_hbm, wo)]
    tail = [load(f_hbm.at[pl.ds(64, ROWS - 64), pl.ds(c * 128, 128)], fb.at[pl.ds(c * ROWS + 64, ROWS - 64), :]) for c in range(C)]
    ks = [load(k_hbm.at[:, pl.ds(c * 128, 128)], kb.at[pl.ds(c * LB, LB), :]) for c in range(C)]
    for q in range(NL):
        for f in range(2):
            small.append(load(wi_hbm.at[pl.ds(f * 128 + q * LB, LB), :], wi.at[pl.ds((q * 2 + f) * LB, LB), :]))

    sub = lax.broadcasted_iota(jnp.int32, (8, 128), 0)
    lane = lax.broadcasted_iota(jnp.int32, (LB, 128), 1)
    lane8 = lax.broadcasted_iota(jnp.int32, (8, 128), 1)

    own_rad = pl.ds(pl.multiple_of(l * 64, 64), 64)
    for c in range(C):
        head[c].wait()
        rb[own_rad, pl.ds(c * 128, 128)] = fb[pl.ds(c * ROWS, 64), :].astype(jnp.bfloat16)

    for copy in small:
        copy.wait()
    for h in range(2):
        sun = sun_ref[h].astype(jnp.float32)
        code = sun * (1.0 + cl[pl.ds(h, 1), :].astype(jnp.float32))
        sb[h] = jnp.where(sub == y, jnp.broadcast_to(code, (8, 128)), 0.0)

    for copy in tail:
        copy.wait()
    lo_side = jnp.zeros((LB, 128), jnp.float32)
    hi_side = jnp.zeros((LB, 128), jnp.float32)
    for f in range(F):
        keep = (lane >= 2 * f) & (lane < 2 * f + 2)
        first = fb[pl.ds(f * LB, LB), :]
        last = fb[pl.ds((C - 1) * ROWS + f * LB, LB), :]
        lo_side = jnp.where(keep, pltpu.roll(first, 2 * f, 1) if f else first, lo_side)
        hi_side = jnp.where(keep, pltpu.roll(last, 2 * f + 2, 1), hi_side)
    hs[0] = hi_side
    hs[1] = lo_side

    low = cm[...] & 127
    for q in range(C):
        row = jnp.broadcast_to(low[q : q + 1, :], (128, 128))
        hit = row == lax.broadcasted_iota(jnp.int32, (128, 128), 0)
        onehot[:, pl.ds(q * 128, 128)] = jnp.where(hit, 1.0, 0.0).astype(jnp.bfloat16)

    pl.semaphore_wait(barrier, len(peers))

    def send(src, dst, ssem, rsem, peer):
        copy = pltpu.make_async_remote_copy(
            src_ref=src, dst_ref=dst, send_sem=ssem, recv_sem=rsem, device_id=peer, device_id_type=MESH
        )
        copy.start()
        return copy

    y_out = [
        send(sb.at[((y + d) % NY) // 4], yb.at[d], y_s.at[d], y_r.at[d], y_peer(d)) for d in range(1, NY)
    ]
    rad_out = [
        send(rb.at[own_rad, :], rb.at[own_rad, :], rad_s.at[d], rad_r.at[d], lev_peer(d)) for d in (1, 3, 2)
    ]
    halo_out = [
        send(hs.at[0], hr.at[0], halo_s.at[0], halo_r.at[0], right),
        send(hs.at[1], hr.at[1], halo_s.at[1], halo_r.at[1], left),
    ]

    for copy in ks:
        copy.wait()
    zero = jnp.zeros((8, 128), jnp.float32)

    def down(i, carry):
        k_prev, s_prev, gv, gs = carry
        k = jnp.where(i < LB - 1, kb[pl.ds(i, 8, stride=LB), :], 0.0)
        d = 1.0 + k_prev * s_prev
        r = 1.0 / (d + k)
        rk[i] = r
        rt[i] = k * r
        gv = (jnp.where(i == 0, 1.0, 0.0) + k_prev * gv) * r
        vb[i] = gv
        new = []
        for f in range(F):
            g = (fb[pl.ds(f * LB + i, 8, stride=ROWS), :] + k_prev * gs[f]) * r
            gb[f * LB + i] = g
            new.append(g)
        return k, d * r, gv, tuple(new)

    carry = lax.fori_loop(0, LB, down, (zero, zero, zero, (zero,) * F))
    lasts = carry[3]

    def up(j, carry):
        u, v, xs = carry
        i = LB - 1 - j
        ratio = rt[i]
        u = ratio * u + jnp.where(j == 0, 1.0, 0.0) * rk[i]
        v = vb[i] + ratio * v
        ub[i] = u
        vb[i] = v
        new = []
        for f in range(F):
            x = gb[f * LB + i] + ratio * xs[f]
            gb[f * LB + i] = x
            new.append(x)
        return u, v, tuple(new)

    _, v_first, firsts = lax.fori_loop(0, LB, up, (zero, zero, (zero,) * F))
    for f in range(F):
        ifb[l, f] = firsts[f]
        ifb[l, F + f] = lasts[f]
    ifb[l, 2 * F] = v_first
    ifb[l, 2 * F + 1] = rk[LB - 1]
    ifb[l, 2 * F + 2] = vb[LB - 1]
    ifb[l, 2 * F + 3] = kb[pl.ds(LB - 1, 8, stride=LB), :]

    for copy in y_out:
        copy.wait_recv()
    total = sb[y // 4]
    for d in range(1, NY):
        total = total + yb[d]
    ys[...] = total

    if_out = [send(ifb.at[l], ifb.at[l], if_s.at[d], if_r.at[d], lev_peer(d)) for d in (1, 3, 2)]
    z_out = [send(ys, zb.at[d], z_s.at[d], z_r.at[d], z_peer(d)) for d in range(1, NZC)]

    for copy in halo_out:
        copy.wait_recv()

    def hyper(f, _):
        base = f * LB
        tiles = [pltpu.roll(hr[0], (126 - 2 * f) % 128, 1)]
        tiles += [fb[pl.ds(pl.multiple_of(c * ROWS + base, LB), LB), :] for c in range(C)]
        tiles += [pltpu.roll(hr[1], (128 - 2 * f) % 128, 1)]
        r1 = [pltpu.roll(t, 1, 1) for t in tiles[:-1]]
        r2 = [pltpu.roll(t, 2, 1) for t in tiles[:-1]]
        m1 = [pltpu.roll(t, 127, 1) for t in tiles[1:]]
        m2 = [pltpu.roll(t, 126, 1) for t in tiles[1:]]
        for c in range(C):
            near = jnp.where(lane < 1, r1[c], r1[c + 1]) + jnp.where(lane >= 127, m1[c + 1], m1[c])
            far = jnp.where(lane < 2, r2[c], r2[c + 1]) + jnp.where(lane >= 126, m2[c + 1], m2[c])
            own = tiles[c + 1]
            fourth = (far - 4.0 * near) + 6.0 * own
            nb[pl.ds(pl.multiple_of(c * ROWS + base, LB), LB), :] = -NU_HYPER * fourth - own
        return 0

    lax.fori_loop(0, F, hyper, 0)

    for copy in rad_out:
        copy.wait_recv()

    def network(q, _):
        cols = pl.ds(pl.multiple_of(q * 256, 256), 256)
        hidden = jnp.tanh(dot0(wi[...], rb[:, cols])).astype(jnp.bfloat16)
        heat = dot0(wo[...], hidden)
        hb[pl.ds(pl.multiple_of(q * 256, 256), 128), :] = heat[:, :128]
        hb[pl.ds(pl.multiple_of(q * 256 + 128, 128), 128), :] = heat[:, 128:]
        return 0

    lax.fori_loop(0, COLS // 256, network, 0)

    def heat_down(i, carry):
        k_prev, g = carry
        g = (hb[pl.ds(l * LB + i, 8, stride=128), :] + k_prev * g) * rk[i]
        hy[i] = g
        return kb[pl.ds(i, 8, stride=LB), :], g

    _, heat_last = lax.fori_loop(0, LB, heat_down, (zero, zero), unroll=4)

    def heat_up(j, x):
        i = LB - 1 - j
        x = hy[i] + rt[i] * x
        hy[i] = x
        return x

    heat_first = lax.fori_loop(0, LB, heat_up, zero, unroll=4)
    hib[l, 0] = heat_first
    hib[l, 1] = heat_last

    for copy in z_out:
        copy.wait_recv()
    source = 32 * (y % 4) + zc * 2
    placed = zero
    for d in range(NZC):
        at = ((zc + NZC - d) % NZC) * 8 + l * 2
        moved = pltpu.roll(zb[d] if d else ys[...], (at - source + 256) % 128, 1)
        placed = jnp.where((lane8 >= at) & (lane8 < at + 2), moved, placed)
    xr[l] = placed
    hi_out = [send(hib.at[l], hib.at[l], hi_s.at[d], hi_r.at[d], lev_peer(d)) for d in (1, 3, 2)]
    x_out = [send(xr.at[l], xr.at[l], x_s.at[d], x_r.at[d], lev_peer(d)) for d in (1, 3, 2)]

    def wait_lev(sends):
        for copy in sends:
            copy.wait_recv()

    wait_lev(if_out)
    v1, v2, v3 = (ifb[b, 2 * F] for b in (1, 2, 3))
    u0, u1, u2 = (ifb[b, 2 * F + 1] for b in (0, 1, 2))
    c1, c2 = ifb[1, 2 * F + 2], ifb[2, 2 * F + 2]
    k0, k1, k2 = (ifb[b, 2 * F + 3] for b in (0, 1, 2))
    w0 = 1.0 / (1.0 / k0 + v1 + u0)
    a1 = c1 * w0
    w1 = 1.0 / (1.0 / k1 + v2 + u1 - c1 * a1)
    a2 = c2 * w1
    w2 = 1.0 / (1.0 / k2 + v3 + u2 - c2 * a2)

    def fluxes(first, last):
        t0 = first(1) - last(0)
        t1 = first(2) - last(1) + a1 * t0
        t2 = first(3) - last(2) + a2 * t1
        f2 = t2 * w2
        f1 = (t1 + c2 * f2) * w1
        f0 = (t0 + c1 * f1) * w0
        below = jnp.where(l == 0, f0, jnp.where(l == 1, f1, jnp.where(l == 2, f2, 0.0)))
        above = jnp.where(l == 1, f0, jnp.where(l == 2, f1, jnp.where(l == 3, f2, 0.0)))
        return below, above

    def finish(f):
        rows = pl.ds(pl.multiple_of(f * LB, LB), LB)
        for c in range(C):
            at = pl.ds(pl.multiple_of(c * ROWS + f * LB, LB), LB)
            ob[rows, pl.ds(c * 128, 128)] = (xb[at, :] + nb[at, :]).astype(jnp.bfloat16)
        pltpu.make_async_copy(ob.at[rows, :], out_hbm.at[rows, :], out_sem.at[f]).start()

    def field(f, _):
        below, above = fluxes(lambda b: ifb[b, f], lambda b: ifb[b, F + f])

        def level(i, _):
            x = gb[f * LB + i] + ub[i] * below - vb[i] * above
            xb[pl.ds(f * LB + i, 8, stride=ROWS), :] = x
            return 0

        lax.fori_loop(0, LB, level, 0, unroll=8)
        finish(f)
        return 0

    lax.fori_loop(1, F, field, 0)

    wait_lev(x_out)
    codes = xr[0] + xr[1] + xr[2] + xr[3]
    high = cm[...] >> 7
    placed_codes = zero
    for q in range(C):
        hit = jnp.broadcast_to(high[q : q + 1, :], (8, 128)) == sub
        row = jnp.where(hit, jnp.broadcast_to(codes[q : q + 1, :], (8, 128)), 0.0)
        placed_codes += dot1(row.astype(jnp.bfloat16), onehot[:, pl.ds(q * 128, 128)])
    factor = jnp.where(placed_codes > 1.5, 1.0 - jnp.float32(CLOUD_SHADE), jnp.where(placed_codes > 0.5, 1.0, 0.0))
    wait_lev(hi_out)
    below, above = fluxes(
        lambda b: ifb[b, 0] + factor * hib[b, 0], lambda b: ifb[b, F] + factor * hib[b, 1]
    )

    def level0(i, _):
        x = gb[i] + factor * hy[i] + ub[i] * below - vb[i] * above
        xb[pl.ds(i, 8, stride=ROWS), :] = x
        return 0

    lax.fori_loop(0, LB, level0, 0, unroll=8)
    finish(0)

    for f in range(F):
        rows = pl.ds(f * LB, LB)
        pltpu.make_async_copy(ob.at[rows, :], out_hbm.at[rows, :], out_sem.at[f]).wait()
    for copy in y_out + rad_out + halo_out + if_out + z_out + hi_out + x_out:
        copy.wait_send()


def body(fields, coupling, column_map, sunlit, cloudy, radiation_in, radiation_out):
    f32, bf16 = jnp.float32, jnp.bfloat16
    anywhere = pl.BlockSpec(memory_space=pl.ANY)
    dma = pltpu.SemaphoreType.DMA
    n_loads = 3 * C + 3 + 2 * NL
    out = pl.pallas_call(
        kernel,
        out_shape=jax.ShapeDtypeStruct((ROWS, COLS), bf16),
        in_specs=[anywhere, anywhere, anywhere, pl.BlockSpec(memory_space=pltpu.SMEM)] + [anywhere] * 3,
        out_specs=anywhere,
        scratch_shapes=[
            pltpu.VMEM((C * ROWS, 128), f32),
            pltpu.VMEM((C * LB, 128), f32),
            pltpu.VMEM((8, 128), jnp.int32),
            pltpu.VMEM((2, 128), jnp.int32),
            pltpu.VMEM((256, 256), bf16),
            pltpu.VMEM((256, 128), bf16),
            pltpu.VMEM((256, COLS), bf16),
            pltpu.VMEM((2, LB, 128), f32),
            pltpu.VMEM((2, LB, 128), f32),
            pltpu.VMEM((2, 8, 128), f32),
            pltpu.VMEM((NY, 8, 128), f32),
            pltpu.VMEM((8, 128), f32),
            pltpu.VMEM((NZC, 8, 128), f32),
            pltpu.VMEM((NL, 8, 128), f32),
            pltpu.VMEM((128, COLS), bf16),
            pltpu.VMEM((ROWS, 8, 128), f32),
            pltpu.VMEM((LB, 8, 128), f32),
            pltpu.VMEM((LB, 8, 128), f32),
            pltpu.VMEM((LB, 8, 128), f32),
            pltpu.VMEM((LB, 8, 128), f32),
            pltpu.VMEM((NL, 2 * F + 4, 8, 128), f32),
            pltpu.VMEM((NL, 2, 8, 128), f32),
            pltpu.VMEM((C * 128, 128), f32),
            pltpu.VMEM((LB, 8, 128), f32),
            pltpu.VMEM((C * ROWS, 128), f32),
            pltpu.VMEM((C * ROWS, 128), f32),
            pltpu.VMEM((ROWS, COLS), bf16),
            dma((n_loads,)), dma((F,)),
            dma((NY,)), dma((NY,)), dma((NZC,)), dma((NZC,)), dma((NL,)), dma((NL,)),
            dma((NL,)), dma((NL,)), dma((2,)), dma((2,)), dma((NL,)), dma((NL,)), dma((NL,)), dma((NL,)),
        ],
        compiler_params=pltpu.CompilerParams(collective_id=0, has_side_effects=True),
        name="column_step",
    )(
        fields.reshape(ROWS, COLS), coupling, column_map.reshape(8, 128), sunlit,
        cloudy.reshape(2, 128), radiation_in, radiation_out,
    )
    return out.reshape(F, LB, COLS)


def solution(mesh):
    placed = (
        P(None, "lev", "elem"),
        P("lev", "elem"),
        P("elem"),
        P(("elem", "lev")),
        P(("elem", "lev")),
        P(),
        P(),
    )
    return jax.shard_map(
        body, mesh=mesh, in_specs=placed, out_specs=P(None, "lev", "elem"), check_vma=False
    )
```

```python
import functools

import jax
import jax.numpy as jnp
from jax import lax
from jax.experimental import pallas as pl
from jax.experimental.pallas import tpu as pltpu
from jax.sharding import PartitionSpec as P

NU_HYPER = 0.05
CLOUD_SHADE = 0.6
MESH = pl.DeviceIdType.MESH

F = 10
NL = 4
NY = 8
NZC = 16
NE = NY * NZC
LB = 32
LT = LB // 8
HALF = LB // 2
COLS = 1024
C = COLS // 128
ROWS = F * LB * C
NIF = 2 * F + 4
PIECES = 10


def dot0(a, b):
    return lax.dot_general(a, b, (((0,), (0,)), ((), ())), preferred_element_type=jnp.float32)


def dot1(a, b):
    return lax.dot_general(a, b, (((1,), (1,)), ((), ())), preferred_element_type=jnp.float32)


def kernel(
    f_hbm, k_hbm, cm_hbm, sun_hbm, cl_hbm, wi_hbm, wo_hbm, ob,
    fb, kb, cm, sun, cl, wi, wo, wit, wot, rb, hs, hr, ht, code, rows2, yb, zb, xr, onehot,
    gb, rk, rt, ub, vb, ifb, hib, hb, hy, xb, nb,
    load_sem, x_sem, y_sem, z_sem, rad_sem, halo_sem, if_sem, hi_sem,
):
    f32, bf16 = jnp.float32, jnp.bfloat16
    e = lax.axis_index("elem")
    l = lax.axis_index("lev")
    y, zc = e // NZC, e % NZC

    def lev_peer(d):
        return (e, (l + d) % NL)

    def y_peer(d):
        return (((y + d) % NY) * NZC + zc, l)

    def z_peer(d):
        return (y * NZC + (zc + d) % NZC, l)

    right, left = ((e + 1) % NE, l), ((e + NE - 1) % NE, l)

    def load(src, dst, i):
        copy = pltpu.make_async_copy(src, dst, load_sem.at[i])
        copy.start()
        return copy

    def wait_all(ref, sem):
        pltpu.make_async_copy(ref, ref, sem).wait()

    flags_in = [load(cl_hbm, cl, 0), load(sun_hbm, sun, 1)]

    barrier = pltpu.get_barrier_semaphore()
    peers = [z_peer(d) for d in range(1, NZC)] + [y_peer(d) for d in range(1, NY)]
    peers += [lev_peer(d) for d in range(1, NL)] + [right, left]
    for peer in peers:
        pl.semaphore_signal(barrier, inc=1, device_id=peer, device_id_type=MESH)

    n_head = 2 * LB * C
    head = load(f_hbm.at[pl.ds(0, n_head), :], fb.at[pl.ds(0, n_head), :], 2)
    tail = load(f_hbm.at[pl.ds(n_head, ROWS - n_head), :], fb.at[pl.ds(n_head, ROWS - n_head), :], 3)
    k_in = load(k_hbm, kb, 4)
    small = [load(cm_hbm, cm, 5), load(wo_hbm, wo, 6)]
    for q in range(NL):
        for f in range(2):
            load(wi_hbm.at[pl.ds(f * 128 + q * LB, LB), :], wi.at[pl.ds((q * 2 + f) * LB, LB), :], 7)

    def send(src, dst, ssem, rsem, peer):
        copy = pltpu.make_async_remote_copy(
            src_ref=src, dst_ref=dst, send_sem=ssem, recv_sem=rsem, device_id=peer, device_id_type=MESH
        )
        copy.start()
        return copy

    for copy in flags_in:
        copy.wait()
    for h in range(2):
        code[pl.ds(h, 1), :] = sun[h].astype(f32) * (1.0 + cl[pl.ds(h, 1), :].astype(f32))

    own_rad = pl.multiple_of(l * 2 * LB, 2 * LB)
    head.wait()
    for f in range(2):
        for t in range(0, LT, 2):
            for c in range(C):
                at = [((f * LT + t + i) * C + c) * 8 for i in range(2)]
                pair = jnp.concatenate([fb[pl.ds(a, 8), :] for a in at], axis=0)
                rb[pl.ds(own_rad + f * LB + t * 8, 16), pl.ds(c * 128, 128)] = pair.astype(bf16)

    sub = lax.broadcasted_iota(jnp.int32, (8, 128), 0)
    lane = lax.broadcasted_iota(jnp.int32, (8, 128), 1)
    tail.wait()
    for t in range(LT):
        lo_side = hi_side = jnp.zeros((8, 128), f32)
        for f in range(F):
            keep = (lane >= 2 * f) & (lane < 2 * f + 2)
            first = fb[pl.ds((f * LT + t) * C * 8, 8), :]
            last = fb[pl.ds(((f * LT + t) * C + C - 1) * 8, 8), :]
            lo_side = jnp.where(keep, pltpu.roll(first, 2 * f, 1) if f else first, lo_side)
            hi_side = jnp.where(keep, pltpu.roll(last, 2 * f + 2, 1), hi_side)
        hs[0, pl.ds(t * 8, 8), :] = hi_side
        hs[1, pl.ds(t * 8, 8), :] = lo_side

    zero = jnp.zeros((8, 128), f32)

    def at_level(f, i):
        return pl.ds((f * LT + i // 8) * C * 8 + i % 8, 8, stride=8)

    k_in.wait()

    def inward(j, carry):
        ka_prev, kb_prev, sa, sb, gv, gu, gas, gbs = carry
        a, b = j, LB - 1 - j
        ka, kb_ = kb[at_level(0, a), :], kb[at_level(0, b - 1), :]
        da, db = 1.0 + ka_prev * sa, 1.0 + kb_prev * sb
        ra, r_b = 1.0 / (da + ka), 1.0 / (db + kb_)
        rk[a], rk[b] = ra, r_b
        rt[a], rt[b] = ka * ra, kb_ * r_b
        start = jnp.where(j == 0, 1.0, 0.0)
        gv = (start + ka_prev * gv) * ra
        gu = (start + kb_prev * gu) * r_b
        vb[a], ub[b] = gv, gu
        new_a, new_b = [], []
        for f in range(F):
            ga = (fb[at_level(f, a), :] + ka_prev * gas[f]) * ra
            g_b = (fb[at_level(f, b), :] + kb_prev * gbs[f]) * r_b
            gb[f * LB + a], gb[f * LB + b] = ga, g_b
            new_a.append(ga)
            new_b.append(g_b)
        return ka, kb_, da * ra, db * r_b, gv, gu, tuple(new_a), tuple(new_b)

    carry = (zero,) * 6 + ((zero,) * F, (zero,) * F)
    for j in range(HALF):
        carry = inward(j, carry)
    _, _, sa, sb, gv, gu, gas, gbs = carry
    up_mid, down_mid = rt[HALF - 1], rt[HALF]
    mid = 1.0 / (sa + sb * up_mid)

    def middle(ga, g_b):
        xa = (ga + up_mid * g_b) * mid
        return xa, g_b + down_mid * xa

    va, v_b = middle(gv, zero)
    ua, u_b = middle(zero, gu)
    vb[HALF - 1], vb[HALF], ub[HALF - 1], ub[HALF] = va, v_b, ua, u_b
    xas, xbs = [], []
    for f in range(F):
        xa, x_b = middle(gas[f], gbs[f])
        gb[f * LB + HALF - 1], gb[f * LB + HALF] = xa, x_b
        xas.append(xa)
        xbs.append(x_b)
    for j in range(HALF - 2, -1, -1):
        a, b = j, LB - 1 - j
        ratio_a, ratio_b = rt[a], rt[b]
        va, v_b = vb[a] + ratio_a * va, ratio_b * v_b
        ua, u_b = ratio_a * ua, ub[b] + ratio_b * u_b
        vb[a], vb[b], ub[a], ub[b] = va, v_b, ua, u_b
        for f in range(F):
            xas[f] = gb[f * LB + a] + ratio_a * xas[f]
            xbs[f] = gb[f * LB + b] + ratio_b * xbs[f]
            gb[f * LB + a], gb[f * LB + b] = xas[f], xbs[f]
    for f in range(F):
        ifb[l, f] = xas[f]
        ifb[l, F + f] = xbs[f]
    ifb[l, 2 * F] = va
    ifb[l, 2 * F + 1] = u_b
    ifb[l, 2 * F + 2] = v_b
    ifb[l, 2 * F + 3] = kb[at_level(0, LB - 1), :]

    def ring_halves(ref_of, sem):
        for i, (d, h) in enumerate(((1, 0), (NL - 1, 1), (1, 1), (NL - 1, 0))):
            own = ref_of(l, h)
            send(own, own, sem.at[0], sem.at[min(i + 1, 3)], lev_peer(d))

    def ring_relay(ref_of, sem):
        for i, (d, h) in enumerate(((1, 0), (NL - 1, 1))):
            ref = ref_of((l + NL - d) % NL, h)
            wait_all(ref, sem.at[1 + i])
            send(ref, ref, sem.at[0], sem.at[3], lev_peer(d))

    def rad_of(q, h):
        return rb.at[pl.ds(pl.multiple_of((q * 2 + h) * LB, LB), LB), :]

    def if_of(q, h):
        return ifb.at[q, pl.ds(h * (NIF // 2), NIF // 2)]

    pl.semaphore_wait(barrier, len(peers))

    for d in range(1, NZC):
        send(code, zb.at[d], z_sem.at[0], z_sem.at[1], z_peer(d))

    ring_halves(rad_of, rad_sem)
    send(hs.at[0], hr.at[0], halo_sem.at[0], halo_sem.at[1], right)
    send(hs.at[1], hr.at[1], halo_sem.at[0], halo_sem.at[1], left)

    for copy in small:
        copy.wait()
    wait_all(wi, load_sem.at[7])
    wit[...] = wi[...].T
    wot[...] = wo[...].T
    row_i = lax.broadcasted_iota(jnp.int32, (128, 128), 0)
    lane_i = lax.broadcasted_iota(jnp.int32, (128, 128), 1)
    wanted = ((lane_i & 31) >> 1) * 8 + (lane_i >> 5) * 2 + (lane_i & 1)
    order = jnp.where(row_i == wanted, 1.0, 0.0).astype(bf16)
    slots = cm[...]
    parts = jnp.concatenate([slots >> 7, slots & 127], axis=0).astype(f32).astype(bf16)
    parts = jnp.dot(parts, order, preferred_element_type=f32)
    high, low = parts[:8], parts[8:]
    row_f = row_i.astype(f32)
    sub_f = sub.astype(f32)
    for q in range(C):
        hit = jnp.broadcast_to(low[q : q + 1, :], (128, 128)) == row_f
        onehot[:, pl.ds(q * 128, 128)] = jnp.where(hit, 1.0, 0.0).astype(bf16)

    ring_relay(rad_of, rad_sem)
    ring_halves(if_of, if_sem)

    wait_all(zb.at[pl.ds(1, NZC - 1)], z_sem.at[1])
    lane2 = lax.broadcasted_iota(jnp.int32, (2, 128), 1)
    mine = (lane2 & 31) >> 1 == zc
    packed = jnp.where(mine, code[...], 0.0)
    for d in range(1, NZC):
        source = (zc + NZC - d) % NZC
        packed += pltpu.roll(jnp.where(mine, zb[d], 0.0), (2 * (source - zc) + 128) % 128, 1)
    for h in range(2):
        rows2[h] = packed[h : h + 1, :]
    for d in range(1, NY):
        send(rows2.at[((y + d) % NY) // 4], yb.at[d], y_sem.at[0], y_sem.at[1], y_peer(d))

    wait_all(rb.at[pl.ds(0, 4 * LB), :], rad_sem.at[3])
    own_out = wot[pl.ds(pl.multiple_of(l * LB, LB), LB), :]

    def network(q, _):
        cols = pl.ds(pl.multiple_of(q * 256, 256), 256)
        hidden = jnp.tanh(jnp.dot(wit[...], rb[:, cols], preferred_element_type=f32)).astype(bf16)
        heat = jnp.dot(own_out, hidden, preferred_element_type=f32)
        for t in range(LT):
            for c in range(2):
                at = pl.multiple_of((t * C + 2 * q + c) * 8, 8)
                hb[pl.ds(at, 8), :] = heat[t * 8 : t * 8 + 8, c * 128 : c * 128 + 128]
        return 0

    lax.fori_loop(0, COLS // 256, network, 0)

    ga = g_b = ka_prev = kb_prev = zero
    for j in range(HALF):
        a, b = j, LB - 1 - j
        ga = (hb[at_level(0, a), :] + ka_prev * ga) * rk[a]
        g_b = (hb[at_level(0, b), :] + kb_prev * g_b) * rk[b]
        hy[a], hy[b] = ga, g_b
        ka_prev, kb_prev = kb[at_level(0, a), :], kb[at_level(0, b - 1), :]
    xa, x_b = middle(ga, g_b)
    hy[HALF - 1], hy[HALF] = xa, x_b
    for j in range(HALF - 2, -1, -1):
        a, b = j, LB - 1 - j
        xa, x_b = hy[a] + rt[a] * xa, hy[b] + rt[b] * x_b
        hy[a], hy[b] = xa, x_b
    hib[l, 0] = xa
    hib[l, 1] = x_b

    for d in (1, 3, 2):
        send(hib.at[l], hib.at[l], hi_sem.at[0], hi_sem.at[1], lev_peer(d))

    ring_relay(if_of, if_sem)

    wait_all(yb.at[pl.ds(1, NY - 1)], y_sem.at[1])
    rows = zero
    for d in range(NY):
        row = yb[d] if d else rows2[y // 4]
        rows = jnp.where(sub == (y + NY - d) % NY, jnp.broadcast_to(row, (8, 128)), rows)
    moved = pltpu.roll(rows, (32 * (l - y % 4) + 128) % 128, 1)
    xr[l] = jnp.where(lane // 32 == l, moved, 0.0)
    for d in (1, 3, 2):
        send(xr.at[l], xr.at[l], x_sem.at[0], x_sem.at[1], lev_peer(d))

    wait_all(hr, halo_sem.at[1])

    for f in range(F):
        for t in range(LT):
            side, at = pl.ds(t * 8, 8), pl.ds((f * LT + t) * 8, 8)
            ht[0, at, :] = pltpu.roll(hr[0, side, :], (126 - 2 * f) % 128, 1)
            ht[1, at, :] = pltpu.roll(hr[1, side, :], (128 - 2 * f) % 128, 1) if f else hr[1, side, :]

    def hyper(f, _):
        for t in range(LT):
            base = pl.multiple_of((f * LT + t) * (C * 8), C * 8)
            side = pl.ds(pl.multiple_of((f * LT + t) * 8, 8), 8)
            tiles = [ht[0, side, :]] + [fb[pl.ds(base + c * 8, 8), :] for c in range(C)] + [ht[1, side, :]]
            r1 = [pltpu.roll(v, 1, 1) for v in tiles[:-1]]
            r2 = [pltpu.roll(v, 2, 1) for v in tiles[:-1]]
            m1 = [pltpu.roll(v, 127, 1) for v in tiles[1:]]
            m2 = [pltpu.roll(v, 126, 1) for v in tiles[1:]]
            for c in range(C):
                near = jnp.where(lane < 1, r1[c], r1[c + 1]) + jnp.where(lane >= 127, m1[c + 1], m1[c])
                far = jnp.where(lane < 2, r2[c], r2[c + 1]) + jnp.where(lane >= 126, m2[c + 1], m2[c])
                own = tiles[c + 1]
                fourth = (far - 4.0 * near) + 6.0 * own
                nb[pl.ds(base + c * 8, 8), :] = -NU_HYPER * fourth - own
        return 0

    lax.fori_loop(0, F, hyper, 0)

    wait_all(ifb.at[pl.ds(0, 2)], if_sem.at[3])
    v1, v2, v3 = (ifb[b, 2 * F] for b in (1, 2, 3))
    u0, u1, u2 = (ifb[b, 2 * F + 1] for b in (0, 1, 2))
    c1, c2 = ifb[1, 2 * F + 2], ifb[2, 2 * F + 2]
    k0, k1, k2 = (ifb[b, 2 * F + 3] for b in (0, 1, 2))
    w0 = 1.0 / (1.0 / k0 + v1 + u0)
    a1 = c1 * w0
    w1 = 1.0 / (1.0 / k1 + v2 + u1 - c1 * a1)
    a2 = c2 * w1
    w2 = 1.0 / (1.0 / k2 + v3 + u2 - c2 * a2)

    def fluxes(first, last):
        t0 = first(1) - last(0)
        t1 = first(2) - last(1) + a1 * t0
        t2 = first(3) - last(2) + a2 * t1
        f2 = t2 * w2
        f1 = (t1 + c2 * f2) * w1
        f0 = (t0 + c1 * f1) * w0
        below = jnp.where(l == 0, f0, jnp.where(l == 1, f1, jnp.where(l == 2, f2, 0.0)))
        above = jnp.where(l == 1, f0, jnp.where(l == 2, f1, jnp.where(l == 3, f2, 0.0)))
        return below, above

    def correct(of, f, below, above):
        base = f * (LB * C)
        for i in range(LB):
            x = of(i) + ub[i] * below - vb[i] * above
            xb[pl.ds(base + (i // 8) * (C * 8) + i % 8, 8, stride=8), :] = x
        return pl.ds(pl.multiple_of(base, LB * C), LB * C)

    def field(f, _):
        below, above = fluxes(lambda b: ifb[b, f], lambda b: ifb[b, F + f])
        rows = correct(lambda i: gb[f * LB + i], f, below, above)
        ob[rows, :] = (xb[rows, :] + nb[rows, :]).astype(bf16)
        return 0

    lax.fori_loop(1, F, field, 0)

    below, above = fluxes(lambda b: ifb[b, 0], lambda b: ifb[b, F])
    rows = correct(lambda i: gb[i], 0, below, above)
    nb[rows, :] = xb[rows, :] + nb[rows, :]
    wait_all(hib.at[pl.ds(0, NL - 1)], hi_sem.at[1])
    below, above = fluxes(lambda b: hib[b, 0], lambda b: hib[b, 1])
    correct(lambda i: hy[i], 0, below, above)

    wait_all(xr.at[pl.ds(0, NL - 1)], x_sem.at[1])
    codes = (xr[0] + xr[1]) + (xr[2] + xr[3])
    placed = zero
    for q in range(C):
        hit = jnp.broadcast_to(high[q : q + 1, :], (8, 128)) == sub_f
        row = jnp.where(hit, jnp.broadcast_to(codes[q : q + 1, :], (8, 128)), 0.0)
        placed += dot1(row.astype(bf16), onehot[:, pl.ds(q * 128, 128)])
    factor = jnp.where(placed > 1.5, 1.0 - f32(CLOUD_SHADE), jnp.where(placed > 0.5, 1.0, 0.0))
    spread = jnp.concatenate([jnp.broadcast_to(factor[c : c + 1, :], (8, 128)) for c in range(C)], axis=0)
    for t in range(LT):
        rows = pl.ds(t * C * 8, C * 8)
        ob[rows, :] = (nb[rows, :] + spread * xb[rows, :]).astype(bf16)

    wait_all(zb.at[pl.ds(1, NZC - 1)], z_sem.at[0])
    wait_all(yb.at[pl.ds(1, NY - 1)], y_sem.at[0])
    wait_all(xr.at[pl.ds(0, NL - 1)], x_sem.at[0])
    wait_all(rb.at[pl.ds(0, 6 * LB), :], rad_sem.at[0])
    wait_all(hs, halo_sem.at[0])
    wait_all(ifb.at[pl.ds(0, 3)], if_sem.at[0])
    wait_all(hib.at[pl.ds(0, NL - 1)], hi_sem.at[0])


def write_out(src, dst, sem):
    size = ROWS // PIECES
    copies = [
        pltpu.make_async_copy(src.at[pl.ds(i * size, size), :], dst.at[pl.ds(i * size, size), :], sem.at[i])
        for i in range(PIECES)
    ]
    for copy in copies:
        copy.start()
    for copy in copies:
        copy.wait()


def tiled(array):
    return array.reshape(-1, 8, C, 128).transpose(0, 2, 1, 3).reshape(-1, 128)


def body(fields, coupling, column_map, sunlit, cloudy, radiation_in, radiation_out):
    f32, bf16 = jnp.float32, jnp.bfloat16
    anywhere = pl.BlockSpec(memory_space=pl.ANY)
    dma = pltpu.SemaphoreType.DMA
    out = pl.pallas_call(
        kernel,
        out_shape=pltpu.VMEM((ROWS, 128), bf16),
        in_specs=[anywhere] * 7,
        out_specs=pl.BlockSpec(memory_space=pltpu.VMEM),
        scratch_shapes=[
            pltpu.VMEM((ROWS, 128), f32),
            pltpu.VMEM((C * LB, 128), f32),
            pltpu.VMEM((8, 128), jnp.int32),
            pltpu.SMEM((2,), jnp.int32),
            pltpu.VMEM((2, 128), jnp.int32),
            pltpu.VMEM((256, 256), bf16),
            pltpu.VMEM((256, 128), bf16),
            pltpu.VMEM((256, 256), bf16),
            pltpu.VMEM((128, 256), bf16),
            pltpu.VMEM((256, COLS), bf16),
            pltpu.VMEM((2, LB, 128), f32),
            pltpu.VMEM((2, LB, 128), f32),
            pltpu.VMEM((2, F * LB, 128), f32),
            pltpu.VMEM((2, 128), f32),
            pltpu.VMEM((2, 1, 128), f32),
            pltpu.VMEM((NY, 1, 128), f32),
            pltpu.VMEM((NZC, 2, 128), f32),
            pltpu.VMEM((NL, 8, 128), f32),
            pltpu.VMEM((128, COLS), bf16),
            pltpu.VMEM((F * LB, 8, 128), f32),
            pltpu.VMEM((LB, 8, 128), f32),
            pltpu.VMEM((LB, 8, 128), f32),
            pltpu.VMEM((LB, 8, 128), f32),
            pltpu.VMEM((LB, 8, 128), f32),
            pltpu.VMEM((NL, NIF, 8, 128), f32),
            pltpu.VMEM((NL, 2, 8, 128), f32),
            pltpu.VMEM((LB * C, 128), f32),
            pltpu.VMEM((LB, 8, 128), f32),
            pltpu.VMEM((ROWS, 128), f32),
            pltpu.VMEM((ROWS, 128), f32),
            dma((8,)), dma((2,)), dma((2,)), dma((2,)), dma((4,)), dma((2,)), dma((4,)), dma((2,)),
        ],
        compiler_params=pltpu.CompilerParams(collective_id=0, has_side_effects=True),
        name="column_step",
    )(
        tiled(fields), tiled(coupling), column_map.reshape(8, 128), sunlit,
        cloudy.reshape(2, 128), radiation_in, radiation_out,
    )
    out = pl.pallas_call(
        write_out,
        out_shape=jax.ShapeDtypeStruct((ROWS, 128), bf16),
        in_specs=[pl.BlockSpec(memory_space=pltpu.VMEM)],
        out_specs=anywhere,
        scratch_shapes=[dma((PIECES,))],
        name="write_out",
    )(pltpu.with_memory_space_constraint(out, pltpu.VMEM))
    return out.reshape(F * LT, C, 8, 128).transpose(0, 2, 1, 3).reshape(F, LB, COLS)


def solution(mesh):
    placed = (
        P(None, "lev", "elem"),
        P("lev", "elem"),
        P("elem"),
        P(("elem", "lev")),
        P(("elem", "lev")),
        P(),
        P(),
    )
    return jax.shard_map(
        body, mesh=mesh, in_specs=placed, out_specs=P(None, "lev", "elem"), check_vma=False
    )
```

```python
import functools

import jax
import jax.numpy as jnp
from jax import lax
from jax.experimental import pallas as pl
from jax.experimental.pallas import tpu as pltpu
from jax.sharding import PartitionSpec as P

NU_HYPER = 0.05
CLOUD_SHADE = 0.6
MESH = pl.DeviceIdType.MESH

F = 10
NL = 4
NY = 8
NZC = 16
NE = NY * NZC
LB = 32
LT = LB // 8
HALF = LB // 2
COLS = 1024
C = COLS // 128
ROWS = F * LB * C
NIF = F + 2


def dot0(a, b):
    return lax.dot_general(a, b, (((0,), (0,)), ((), ())), preferred_element_type=jnp.float32)


def dot1(a, b):
    return lax.dot_general(a, b, (((1,), (1,)), ((), ())), preferred_element_type=jnp.float32)


def kernel(
    f_hbm, k_hbm, cm_hbm, sun_hbm, cl_hbm, wi_hbm, wo_hbm, ob,
    fb, kb, cm, sun, cl, wi, wo, wit, wot, rb, hs, hr, ht, code, rows2, yb, zb, xr,
    gb, rk, rt, ub, vb, mine_if, next_if, lows, ifb, hib, hb, hy, xb, nb,
    load_sem, x_sem, y_sem, z_sem, rad_sem, halo_sem, near_sem, if_sem, hi_sem,
):
    f32, bf16 = jnp.float32, jnp.bfloat16
    e = lax.axis_index("elem")
    l = lax.axis_index("lev")
    y, zc = e // NZC, e % NZC

    def lev_peer(d):
        return (e, (l + d) % NL)

    def y_peer(d):
        return (((y + d) % NY) * NZC + zc, l)

    def z_peer(d):
        return (y * NZC + (zc + d) % NZC, l)

    right, left = ((e + 1) % NE, l), ((e + NE - 1) % NE, l)

    def load(src, dst, i):
        copy = pltpu.make_async_copy(src, dst, load_sem.at[i])
        copy.start()
        return copy

    def wait_all(ref, sem):
        pltpu.make_async_copy(ref, ref, sem).wait()

    flags_in = [load(cl_hbm, cl, 0), load(sun_hbm, sun, 1)]

    barrier = pltpu.get_barrier_semaphore()
    peers = [y_peer(d) for d in (4, 3, 5, 2, 6, 1, 7)] + [z_peer(d) for d in range(1, NZC)]
    peers += [lev_peer(d) for d in range(1, NL)] + [right, left]
    for peer in peers:
        pl.semaphore_signal(barrier, inc=1, device_id=peer, device_id_type=MESH)

    n_head = 2 * LB * C
    head = load(f_hbm.at[pl.ds(0, n_head), :], fb.at[pl.ds(0, n_head), :], 2)
    tail = load(f_hbm.at[pl.ds(n_head, ROWS - n_head), :], fb.at[pl.ds(n_head, ROWS - n_head), :], 3)
    k_in = load(k_hbm, kb, 4)
    load(cm_hbm, cm, 5)
    load(wo_hbm, wo, 5)
    for q in range(NL):
        for f in range(2):
            load(wi_hbm.at[pl.ds(f * 128 + q * LB, LB), :], wi.at[pl.ds((q * 2 + f) * LB, LB), :], 5)

    def send(src, dst, ssem, rsem, peer):
        copy = pltpu.make_async_remote_copy(
            src_ref=src, dst_ref=dst, send_sem=ssem, recv_sem=rsem, device_id=peer, device_id_type=MESH
        )
        copy.start()
        return copy

    for copy in flags_in:
        copy.wait()
    for h in range(2):
        code[pl.ds(h, 1), :] = sun[h].astype(f32) * (1.0 + cl[pl.ds(h, 1), :].astype(f32))

    own_rad = pl.multiple_of(l * 2 * LB, 2 * LB)
    head.wait()
    for f in range(2):
        for t in range(0, LT, 2):
            for c in range(C):
                at = [((f * LT + t + i) * C + c) * 8 for i in range(2)]
                pair = jnp.concatenate([fb[pl.ds(a, 8), :] for a in at], axis=0)
                rb[pl.ds(own_rad + f * LB + t * 8, 16), pl.ds(c * 128, 128)] = pair.astype(bf16)

    def ring_halves(ref_of, sem):
        for i, (d, h) in enumerate(((1, 0), (NL - 1, 1), (1, 1), (NL - 1, 0))):
            own = ref_of(l, h)
            send(own, own, sem.at[0], sem.at[min(i + 1, 3)], lev_peer(d))

    def ring_relay(ref_of, sem):
        for i, (d, h) in enumerate(((1, 0), (NL - 1, 1))):
            ref = ref_of((l + NL - d) % NL, h)
            wait_all(ref, sem.at[1 + i])
            send(ref, ref, sem.at[0], sem.at[3], lev_peer(d))

    def rad_of(q, h):
        return rb.at[pl.ds(pl.multiple_of((q * 2 + h) * LB, LB), LB), :]

    pl.semaphore_wait(barrier, len(peers))

    for d in range(1, NZC):
        send(code, zb.at[d], z_sem.at[0], z_sem.at[1], z_peer(d))

    ring_halves(rad_of, rad_sem)
    sub = lax.broadcasted_iota(jnp.int32, (8, 128), 0)
    lane = lax.broadcasted_iota(jnp.int32, (8, 128), 1)

    tail.wait()
    for t in range(LT):
        lo_side = hi_side = jnp.zeros((8, 128), f32)
        for f in range(F):
            keep = (lane >= 2 * f) & (lane < 2 * f + 2)
            first = fb[pl.ds((f * LT + t) * C * 8, 8), :]
            last = fb[pl.ds(((f * LT + t) * C + C - 1) * 8, 8), :]
            lo_side = jnp.where(keep, pltpu.roll(first, 2 * f, 1) if f else first, lo_side)
            hi_side = jnp.where(keep, pltpu.roll(last, 2 * f + 2, 1), hi_side)
        hs[0, pl.ds(t * 8, 8), :] = hi_side
        hs[1, pl.ds(t * 8, 8), :] = lo_side
    send(hs.at[0], hr.at[0], halo_sem.at[0], halo_sem.at[1], right)
    send(hs.at[1], hr.at[1], halo_sem.at[0], halo_sem.at[1], left)

    zero = jnp.zeros((8, 128), f32)

    def at_level(f, i):
        return pl.ds((f * LT + i // 8) * C * 8 + i % 8, 8, stride=8)

    k_in.wait()

    def inward(j, carry):
        ka_prev, kb_prev, sa, sb, gv, gu, gas, gbs = carry
        a, b = j, LB - 1 - j
        ka, kb_ = kb[at_level(0, a), :], kb[at_level(0, b - 1), :]
        da, db = 1.0 + ka_prev * sa, 1.0 + kb_prev * sb
        ra, r_b = 1.0 / (da + ka), 1.0 / (db + kb_)
        rk[a], rk[b] = ra, r_b
        rt[a], rt[b] = ka * ra, kb_ * r_b
        start = jnp.where(j == 0, 1.0, 0.0)
        gv = (start + ka_prev * gv) * ra
        gu = (start + kb_prev * gu) * r_b
        vb[a], ub[b] = gv, gu
        new_a, new_b = [], []
        for f in range(F):
            ga = (fb[at_level(f, a), :] + ka_prev * gas[f]) * ra
            g_b = (fb[at_level(f, b), :] + kb_prev * gbs[f]) * r_b
            gb[f * LB + a], gb[f * LB + b] = ga, g_b
            new_a.append(ga)
            new_b.append(g_b)
        return ka, kb_, da * ra, db * r_b, gv, gu, tuple(new_a), tuple(new_b)

    carry = (zero,) * 6 + ((zero,) * F, (zero,) * F)
    for j in range(HALF):
        carry = inward(j, carry)
    _, _, sa, sb, gv, gu, gas, gbs = carry
    up_mid, down_mid = rt[HALF - 1], rt[HALF]
    mid = 1.0 / (sa + sb * up_mid)

    def middle(ga, g_b):
        xa = (ga + up_mid * g_b) * mid
        return xa, g_b + down_mid * xa

    va, v_b = middle(gv, zero)
    ua, u_b = middle(zero, gu)
    vb[HALF - 1], vb[HALF], ub[HALF - 1], ub[HALF] = va, v_b, ua, u_b
    xas, xbs = [], []
    for f in range(F):
        xa, x_b = middle(gas[f], gbs[f])
        gb[f * LB + HALF - 1], gb[f * LB + HALF] = xa, x_b
        xas.append(xa)
        xbs.append(x_b)
    for j in range(HALF - 2, -1, -1):
        a, b = j, LB - 1 - j
        ratio_a, ratio_b = rt[a], rt[b]
        va, v_b = vb[a] + ratio_a * va, ratio_b * v_b
        ua, u_b = ratio_a * ua, ub[b] + ratio_b * u_b
        vb[a], vb[b], ub[a], ub[b] = va, v_b, ua, u_b
        for f in range(F):
            xas[f] = gb[f * LB + a] + ratio_a * xas[f]
            xbs[f] = gb[f * LB + b] + ratio_b * xbs[f]
            gb[f * LB + a], gb[f * LB + b] = xas[f], xbs[f]
    for f in range(F):
        mine_if[f] = xas[f]
        lows[f] = xbs[f]
    mine_if[F] = va
    lows[F] = u_b + 1.0 / kb[at_level(0, LB - 1), :]
    send(mine_if, next_if, near_sem.at[0], near_sem.at[1], lev_peer(NL - 1))

    wait_all(fb.at[pl.ds(0, 8 + 128 + 256), :], load_sem.at[5])
    wit[...] = wi[...].T
    wot[...] = wo[...].T
    row_i = lax.broadcasted_iota(jnp.int32, (128, 128), 0)
    lane_i = lax.broadcasted_iota(jnp.int32, (128, 128), 1)
    wanted = ((lane_i & 31) >> 1) * 8 + (lane_i >> 5) * 2 + (lane_i & 1)
    order = jnp.where(row_i == wanted, 1.0, 0.0).astype(bf16)
    slots = cm[...]
    parts = jnp.concatenate([slots >> 7, slots & 127], axis=0).astype(f32).astype(bf16)
    parts = jnp.dot(parts, order, preferred_element_type=f32)
    high, low = parts[:8], parts[8:]
    row_f = row_i.astype(f32)
    sub_f, lane_f = sub.astype(f32), lane.astype(f32)
    found = jnp.zeros((16, 128), f32)
    for q in range(C):
        hit = jnp.broadcast_to(low[q : q + 1, :], (128, 128)) == row_f
        onehot = jnp.where(hit, 1.0, 0.0).astype(bf16)
        here = jnp.broadcast_to(high[q : q + 1, :], (8, 128)) == sub_f
        slot = jnp.concatenate([jnp.where(here, float(q), 0.0), jnp.where(here, lane_f, 0.0)], axis=0)
        found += dot1(slot.astype(bf16), onehot)
    row_at, lane_at = found[:8].astype(jnp.int32), found[8:].astype(jnp.int32)

    ring_relay(rad_of, rad_sem)

    wait_all(zb.at[pl.ds(1, NZC - 1)], z_sem.at[1])
    lane2 = lax.broadcasted_iota(jnp.int32, (2, 128), 1)
    mine = (lane2 & 31) >> 1 == zc
    packed = jnp.where(mine, code[...], 0.0)
    for d in range(1, NZC):
        source = (zc + NZC - d) % NZC
        packed += pltpu.roll(jnp.where(mine, zb[d], 0.0), (2 * (source - zc) + 128) % 128, 1)
    for h in range(2):
        rows2[h] = packed[h : h + 1, :]
    for d in range(1, NY):
        send(rows2.at[((y + d) % NY) // 4], yb.at[d], y_sem.at[0], y_sem.at[1], y_peer(d))

    wait_all(next_if, near_sem.at[1])
    for f in range(F):
        ifb[l, f] = next_if[f] - lows[f]
    ifb[l, F] = next_if[F] + lows[F]
    ifb[l, F + 1] = v_b
    for d in (2, 1, 3):
        send(ifb.at[l], ifb.at[l], if_sem.at[0], if_sem.at[1], lev_peer(d))

    wait_all(hr, halo_sem.at[1])

    for f in range(F):
        for t in range(LT):
            side, at = pl.ds(t * 8, 8), pl.ds((f * LT + t) * 8, 8)
            ht[0, at, :] = pltpu.roll(hr[0, side, :], (126 - 2 * f) % 128, 1)
            ht[1, at, :] = pltpu.roll(hr[1, side, :], (128 - 2 * f) % 128, 1) if f else hr[1, side, :]

    def hyper(f, _):
        for t in range(LT):
            base = pl.multiple_of((f * LT + t) * (C * 8), C * 8)
            side = pl.ds(pl.multiple_of((f * LT + t) * 8, 8), 8)
            tiles = [ht[0, side, :]] + [fb[pl.ds(base + c * 8, 8), :] for c in range(C)] + [ht[1, side, :]]
            r1 = [pltpu.roll(v, 1, 1) for v in tiles[:-1]]
            r2 = [pltpu.roll(v, 2, 1) for v in tiles[:-1]]
            m1 = [pltpu.roll(v, 127, 1) for v in tiles[1:]]
            m2 = [pltpu.roll(v, 126, 1) for v in tiles[1:]]
            for c in range(C):
                near = jnp.where(lane < 1, r1[c], r1[c + 1]) + jnp.where(lane >= 127, m1[c + 1], m1[c])
                far = jnp.where(lane < 2, r2[c], r2[c + 1]) + jnp.where(lane >= 126, m2[c + 1], m2[c])
                own = tiles[c + 1]
                fourth = (far - 4.0 * near) + 6.0 * own
                nb[pl.ds(base + c * 8, 8), :] = -NU_HYPER * fourth - own
        return 0

    lax.fori_loop(0, F, hyper, 0, unroll=5)

    wait_all(rb.at[pl.ds(0, 4 * LB), :], rad_sem.at[3])
    own_out = wot[pl.ds(pl.multiple_of(l * LB, LB), LB), :]

    def network(q, _):
        cols = pl.ds(pl.multiple_of(q * 256, 256), 256)
        hidden = jnp.tanh(jnp.dot(wit[...], rb[:, cols], preferred_element_type=f32)).astype(bf16)
        heat = jnp.dot(own_out, hidden, preferred_element_type=f32)
        for t in range(LT):
            for c in range(2):
                at = pl.multiple_of((t * C + 2 * q + c) * 8, 8)
                hb[pl.ds(at, 8), :] = heat[t * 8 : t * 8 + 8, c * 128 : c * 128 + 128]
        return 0

    lax.fori_loop(0, COLS // 256, network, 0, unroll=4)

    ga = g_b = ka_prev = kb_prev = zero
    for j in range(HALF):
        a, b = j, LB - 1 - j
        ga = (hb[at_level(0, a), :] + ka_prev * ga) * rk[a]
        g_b = (hb[at_level(0, b), :] + kb_prev * g_b) * rk[b]
        hy[a], hy[b] = ga, g_b
        ka_prev, kb_prev = kb[at_level(0, a), :], kb[at_level(0, b - 1), :]
    xa, x_b = middle(ga, g_b)
    hy[HALF - 1], hy[HALF] = xa, x_b
    for j in range(HALF - 2, -1, -1):
        a, b = j, LB - 1 - j
        xa, x_b = hy[a] + rt[a] * xa, hy[b] + rt[b] * x_b
        hy[a], hy[b] = xa, x_b
    hib[l, 0] = xa
    hib[l, 1] = x_b

    for d in (1, 3, 2):
        send(hib.at[l], hib.at[l], hi_sem.at[0], hi_sem.at[1], lev_peer(d))


    wait_all(yb.at[pl.ds(1, NY - 1)], y_sem.at[1])
    rows = zero
    for d in range(NY):
        row = yb[d] if d else rows2[y // 4]
        rows = jnp.where(sub == (y + NY - d) % NY, jnp.broadcast_to(row, (8, 128)), rows)
    moved = pltpu.roll(rows, (32 * (l - y % 4) + 128) % 128, 1)
    xr[l] = jnp.where(lane // 32 == l, moved, 0.0)
    for d in (1, 3, 2):
        send(xr.at[l], xr.at[l], x_sem.at[0], x_sem.at[1], lev_peer(d))

    wait_all(ifb.at[pl.ds(0, NL - 1)], if_sem.at[1])
    c1, c2 = ifb[1, F + 1], ifb[2, F + 1]
    w0 = 1.0 / ifb[0, F]
    a1 = c1 * w0
    w1 = 1.0 / (ifb[1, F] - c1 * a1)
    a2 = c2 * w1
    w2 = 1.0 / (ifb[2, F] - c2 * a2)

    def fluxes(rise):
        t0 = rise(0)
        t1 = rise(1) + a1 * t0
        t2 = rise(2) + a2 * t1
        f2 = t2 * w2
        f1 = (t1 + c2 * f2) * w1
        f0 = (t0 + c1 * f1) * w0
        below = jnp.where(l == 0, f0, jnp.where(l == 1, f1, jnp.where(l == 2, f2, 0.0)))
        above = jnp.where(l == 1, f0, jnp.where(l == 2, f1, jnp.where(l == 3, f2, 0.0)))
        return below, above

    def correct(of, f, below, above):
        base = f * (LB * C)
        for i in range(LB):
            x = of(i) + ub[i] * below - vb[i] * above
            xb[pl.ds(base + (i // 8) * (C * 8) + i % 8, 8, stride=8), :] = x
        return pl.ds(pl.multiple_of(base, LB * C), LB * C)

    def field(f, _):
        below, above = fluxes(lambda b: ifb[b, f])
        rows = correct(lambda i: gb[f * LB + i], f, below, above)
        ob[rows, :] = (xb[rows, :] + nb[rows, :]).astype(bf16)
        return 0

    lax.fori_loop(1, F, field, 0)

    below, above = fluxes(lambda b: ifb[b, 0])
    rows = correct(lambda i: gb[i], 0, below, above)
    nb[rows, :] = xb[rows, :] + nb[rows, :]
    wait_all(hib.at[pl.ds(0, NL - 1)], hi_sem.at[1])
    below, above = fluxes(lambda b: hib[b + 1, 0] - hib[b, 1])
    correct(lambda i: hy[i], 0, below, above)

    wait_all(xr.at[pl.ds(0, NL - 1)], x_sem.at[1])
    codes = (xr[0] + xr[1]) + (xr[2] + xr[3])
    placed = zero
    for q in range(C):
        row = jnp.broadcast_to(codes[q : q + 1, :], (8, 128))
        placed = jnp.where(row_at == q, jnp.take_along_axis(row, lane_at, axis=1), placed)
    factor = jnp.where(placed > 1.5, 1.0 - f32(CLOUD_SHADE), jnp.where(placed > 0.5, 1.0, 0.0))
    spread = jnp.concatenate([jnp.broadcast_to(factor[c : c + 1, :], (8, 128)) for c in range(C)], axis=0)
    for t in range(LT):
        rows = pl.ds(t * C * 8, C * 8)
        ob[rows, :] = (nb[rows, :] + spread * xb[rows, :]).astype(bf16)

    wait_all(zb.at[pl.ds(1, NZC - 1)], z_sem.at[0])
    wait_all(yb.at[pl.ds(1, NY - 1)], y_sem.at[0])
    wait_all(xr.at[pl.ds(0, NL - 1)], x_sem.at[0])
    wait_all(rb.at[pl.ds(0, 6 * LB), :], rad_sem.at[0])
    wait_all(hs, halo_sem.at[0])
    wait_all(next_if, near_sem.at[0])
    wait_all(ifb.at[pl.ds(0, 3)], if_sem.at[0])
    wait_all(hib.at[pl.ds(0, NL - 1)], hi_sem.at[0])


def tiled(array):
    return array.reshape(-1, 8, C, 128).transpose(0, 2, 1, 3).reshape(-1, 128)


def body(fields, coupling, column_map, sunlit, cloudy, radiation_in, radiation_out):
    f32, bf16 = jnp.float32, jnp.bfloat16
    anywhere = pl.BlockSpec(memory_space=pl.ANY)
    dma = pltpu.SemaphoreType.DMA
    out = pl.pallas_call(
        kernel,
        out_shape=pltpu.VMEM((ROWS, 128), bf16),
        in_specs=[anywhere] * 7,
        out_specs=pl.BlockSpec(memory_space=pltpu.VMEM),
        scratch_shapes=[
            pltpu.VMEM((ROWS, 128), f32),
            pltpu.VMEM((C * LB, 128), f32),
            pltpu.VMEM((8, 128), jnp.int32),
            pltpu.SMEM((2,), jnp.int32),
            pltpu.VMEM((2, 128), jnp.int32),
            pltpu.VMEM((256, 256), bf16),
            pltpu.VMEM((256, 128), bf16),
            pltpu.VMEM((256, 256), bf16),
            pltpu.VMEM((128, 256), bf16),
            pltpu.VMEM((256, COLS), bf16),
            pltpu.VMEM((2, LB, 128), f32),
            pltpu.VMEM((2, LB, 128), f32),
            pltpu.VMEM((2, F * LB, 128), f32),
            pltpu.VMEM((2, 128), f32),
            pltpu.VMEM((2, 1, 128), f32),
            pltpu.VMEM((NY, 1, 128), f32),
            pltpu.VMEM((NZC, 2, 128), f32),
            pltpu.VMEM((NL, 8, 128), f32),
            pltpu.VMEM((F * LB, 8, 128), f32),
            pltpu.VMEM((LB, 8, 128), f32),
            pltpu.VMEM((LB, 8, 128), f32),
            pltpu.VMEM((LB, 8, 128), f32),
            pltpu.VMEM((LB, 8, 128), f32),
            pltpu.VMEM((F + 1, 8, 128), f32),
            pltpu.VMEM((F + 1, 8, 128), f32),
            pltpu.VMEM((F + 1, 8, 128), f32),
            pltpu.VMEM((NL, NIF, 8, 128), f32),
            pltpu.VMEM((NL, 2, 8, 128), f32),
            pltpu.VMEM((LB * C, 128), f32),
            pltpu.VMEM((LB, 8, 128), f32),
            pltpu.VMEM((ROWS, 128), f32),
            pltpu.VMEM((ROWS, 128), f32),
            dma((6,)), dma((2,)), dma((2,)), dma((2,)), dma((4,)), dma((2,)), dma((2,)), dma((2,)), dma((2,)),
        ],
        compiler_params=pltpu.CompilerParams(collective_id=0, has_side_effects=True),
        name="column_step",
    )(
        tiled(fields), tiled(coupling), column_map.reshape(8, 128), sunlit,
        cloudy.reshape(2, 128), radiation_in, radiation_out,
    )
    return out.reshape(F * LT, C, 8, 128).transpose(0, 2, 1, 3).reshape(F, LB, COLS)


def solution(mesh):
    placed = (
        P(None, "lev", "elem"),
        P("lev", "elem"),
        P("elem"),
        P(("elem", "lev")),
        P(("elem", "lev")),
        P(),
        P(),
    )
    return jax.shard_map(
        body, mesh=mesh, in_specs=placed, out_specs=P(None, "lev", "elem"), check_vma=False
    )
```

```python
import functools

import jax
import jax.numpy as jnp
from jax import lax
from jax.experimental import pallas as pl
from jax.experimental.pallas import tpu as pltpu
from jax.sharding import PartitionSpec as P

NU_HYPER = 0.05
CLOUD_SHADE = 0.6
MESH = pl.DeviceIdType.MESH

F = 10
NL = 4
NY = 8
NZC = 16
NE = NY * NZC
LB = 32
LT = LB // 8
HALF = LB // 2
COLS = 1024
C = COLS // 128
ROWS = F * LB * C
NIF = F + 2


def dot0(a, b):
    return lax.dot_general(a, b, (((0,), (0,)), ((), ())), preferred_element_type=jnp.float32)


def dot1(a, b):
    return lax.dot_general(a, b, (((1,), (1,)), ((), ())), preferred_element_type=jnp.float32)


def kernel(
    f_hbm, k_hbm, cm_hbm, sun_hbm, cl_hbm, wi_hbm, wo_hbm, ob,
    fb, kb, cm, sun, cl, wi, wo, wit, wot, rb, hs, hr, ht, code, rows2, ab, zb,
    gb, rk, rt, ub, vb, mine_if, next_if, lows, ifb, hib, hb, hy, xb, nb,
    load_sem, a_sem, z_sem, rad_sem, halo_sem, near_sem, if_sem, hi_sem,
):
    f32, bf16 = jnp.float32, jnp.bfloat16
    e = lax.axis_index("elem")
    l = lax.axis_index("lev")
    y, zc = e // NZC, e % NZC

    def lev_peer(d):
        return (e, (l + d) % NL)

    def plane_peer(dl, dy):
        return (((y + dy) % NY) * NZC + zc, (l + dl) % NL)

    def z_peer(d):
        return (y * NZC + (zc + d) % NZC, l)

    right, left = ((e + 1) % NE, l), ((e + NE - 1) % NE, l)
    plane = [(dl, dy) for dy in (4, 3, 5, 2, 6, 1, 7, 0) for dl in (2, 1, 3, 0) if dl or dy]

    def load(src, dst, i):
        copy = pltpu.make_async_copy(src, dst, load_sem.at[i])
        copy.start()
        return copy

    def wait_all(ref, sem):
        pltpu.make_async_copy(ref, ref, sem).wait()

    flags_in = [load(cl_hbm, cl, 0), load(sun_hbm, sun, 1)]

    barrier = pltpu.get_barrier_semaphore()
    peers = [plane_peer(*d) for d in plane] + [z_peer(d) for d in range(1, NZC)] + [right, left]
    for peer in peers:
        pl.semaphore_signal(barrier, inc=1, device_id=peer, device_id_type=MESH)

    n_head = 2 * LB * C
    head = load(f_hbm.at[pl.ds(0, n_head), :], fb.at[pl.ds(0, n_head), :], 2)
    tail = load(f_hbm.at[pl.ds(n_head, ROWS - n_head), :], fb.at[pl.ds(n_head, ROWS - n_head), :], 3)
    k_in = load(k_hbm, kb, 4)
    load(cm_hbm, cm, 5)
    load(wo_hbm, wo, 5)
    for q in range(NL):
        for f in range(2):
            load(wi_hbm.at[pl.ds(f * 128 + q * LB, LB), :], wi.at[pl.ds((q * 2 + f) * LB, LB), :], 5)

    def send(src, dst, ssem, rsem, peer):
        copy = pltpu.make_async_remote_copy(
            src_ref=src, dst_ref=dst, send_sem=ssem, recv_sem=rsem, device_id=peer, device_id_type=MESH
        )
        copy.start()
        return copy

    for copy in flags_in:
        copy.wait()
    for h in range(2):
        code[pl.ds(h, 1), :] = sun[h].astype(f32) * (1.0 + cl[pl.ds(h, 1), :].astype(f32))

    own_rad = pl.multiple_of(l * 2 * LB, 2 * LB)
    head.wait()
    for f in range(2):
        for t in range(0, LT, 2):
            for c in range(C):
                at = [((f * LT + t + i) * C + c) * 8 for i in range(2)]
                pair = jnp.concatenate([fb[pl.ds(a, 8), :] for a in at], axis=0)
                rb[pl.ds(own_rad + f * LB + t * 8, 16), pl.ds(c * 128, 128)] = pair.astype(bf16)

    def ring_halves(ref_of, sem):
        for i, (d, h) in enumerate(((1, 0), (NL - 1, 1), (1, 1), (NL - 1, 0))):
            own = ref_of(l, h)
            send(own, own, sem.at[0], sem.at[min(i + 1, 3)], lev_peer(d))

    def ring_relay(ref_of, sem):
        for i, (d, h) in enumerate(((1, 0), (NL - 1, 1))):
            ref = ref_of((l + NL - d) % NL, h)
            wait_all(ref, sem.at[1 + i])
            send(ref, ref, sem.at[0], sem.at[3], lev_peer(d))

    def rad_of(q, h):
        return rb.at[pl.ds(pl.multiple_of((q * 2 + h) * LB, LB), LB), :]

    pl.semaphore_wait(barrier, len(peers))

    for d in range(1, NZC):
        send(code, zb.at[d], z_sem.at[0], z_sem.at[1], z_peer(d))

    ring_halves(rad_of, rad_sem)
    sub = lax.broadcasted_iota(jnp.int32, (8, 128), 0)
    lane = lax.broadcasted_iota(jnp.int32, (8, 128), 1)

    tail.wait()
    for t in range(LT):
        lo_side = hi_side = jnp.zeros((8, 128), f32)
        for f in range(F):
            keep = (lane >= 2 * f) & (lane < 2 * f + 2)
            first = fb[pl.ds((f * LT + t) * C * 8, 8), :]
            last = fb[pl.ds(((f * LT + t) * C + C - 1) * 8, 8), :]
            lo_side = jnp.where(keep, pltpu.roll(first, 2 * f, 1) if f else first, lo_side)
            hi_side = jnp.where(keep, pltpu.roll(last, 2 * f + 2, 1), hi_side)
        hs[0, pl.ds(t * 8, 8), :] = hi_side
        hs[1, pl.ds(t * 8, 8), :] = lo_side
    send(hs.at[0], hr.at[0], halo_sem.at[0], halo_sem.at[1], right)
    send(hs.at[1], hr.at[1], halo_sem.at[0], halo_sem.at[1], left)

    zero = jnp.zeros((8, 128), f32)

    def at_level(f, i):
        return pl.ds((f * LT + i // 8) * C * 8 + i % 8, 8, stride=8)

    k_in.wait()

    def inward(j, carry):
        ka_prev, kb_prev, sa, sb, gv, gu, gas, gbs = carry
        a, b = j, LB - 1 - j
        ka, kb_ = kb[at_level(0, a), :], kb[at_level(0, b - 1), :]
        da, db = 1.0 + ka_prev * sa, 1.0 + kb_prev * sb
        ra, r_b = 1.0 / (da + ka), 1.0 / (db + kb_)
        rk[a], rk[b] = ra, r_b
        rt[a], rt[b] = ka * ra, kb_ * r_b
        start = jnp.where(j == 0, 1.0, 0.0)
        gv = (start + ka_prev * gv) * ra
        gu = (start + kb_prev * gu) * r_b
        vb[a], ub[b] = gv, gu
        new_a, new_b = [], []
        for f in range(F):
            ga = (fb[at_level(f, a), :] + ka_prev * gas[f]) * ra
            g_b = (fb[at_level(f, b), :] + kb_prev * gbs[f]) * r_b
            gb[f * LB + a], gb[f * LB + b] = ga, g_b
            new_a.append(ga)
            new_b.append(g_b)
        return ka, kb_, da * ra, db * r_b, gv, gu, tuple(new_a), tuple(new_b)

    carry = (zero,) * 6 + ((zero,) * F, (zero,) * F)
    for j in range(HALF):
        carry = inward(j, carry)
    _, _, sa, sb, gv, gu, gas, gbs = carry
    up_mid, down_mid = rt[HALF - 1], rt[HALF]
    mid = 1.0 / (sa + sb * up_mid)

    def middle(ga, g_b):
        xa = (ga + up_mid * g_b) * mid
        return xa, g_b + down_mid * xa

    va, v_b = middle(gv, zero)
    ua, u_b = middle(zero, gu)
    vb[HALF - 1], vb[HALF], ub[HALF - 1], ub[HALF] = va, v_b, ua, u_b
    xas, xbs = [], []
    for f in range(F):
        xa, x_b = middle(gas[f], gbs[f])
        gb[f * LB + HALF - 1], gb[f * LB + HALF] = xa, x_b
        xas.append(xa)
        xbs.append(x_b)
    for j in range(HALF - 2, -1, -1):
        a, b = j, LB - 1 - j
        ratio_a, ratio_b = rt[a], rt[b]
        va, v_b = vb[a] + ratio_a * va, ratio_b * v_b
        ua, u_b = ratio_a * ua, ub[b] + ratio_b * u_b
        vb[a], vb[b], ub[a], ub[b] = va, v_b, ua, u_b
        for f in range(F):
            xas[f] = gb[f * LB + a] + ratio_a * xas[f]
            xbs[f] = gb[f * LB + b] + ratio_b * xbs[f]
            gb[f * LB + a], gb[f * LB + b] = xas[f], xbs[f]
    for f in range(F):
        mine_if[f] = xas[f]
        lows[f] = xbs[f]
    mine_if[F] = va
    lows[F] = u_b + 1.0 / kb[at_level(0, LB - 1), :]
    send(mine_if, next_if, near_sem.at[0], near_sem.at[1], lev_peer(NL - 1))

    wait_all(fb.at[pl.ds(0, 8 + 128 + 256), :], load_sem.at[5])
    wit[...] = wi[...].T
    wot[...] = wo[...].T
    row_i = lax.broadcasted_iota(jnp.int32, (128, 128), 0)
    lane_i = lax.broadcasted_iota(jnp.int32, (128, 128), 1)
    wanted = ((lane_i & 31) >> 1) * 8 + (lane_i >> 5) * 2 + (lane_i & 1)
    order = jnp.where(row_i == wanted, 1.0, 0.0).astype(bf16)
    slots = cm[...]
    parts = jnp.concatenate([slots >> 7, slots & 127], axis=0).astype(f32).astype(bf16)
    parts = jnp.dot(parts, order, preferred_element_type=f32)
    high, low = parts[:8], parts[8:]
    row_f = row_i.astype(f32)
    sub_f, lane_f = sub.astype(f32), lane.astype(f32)
    found = jnp.zeros((16, 128), f32)
    for q in range(C):
        hit = jnp.broadcast_to(low[q : q + 1, :], (128, 128)) == row_f
        onehot = jnp.where(hit, 1.0, 0.0).astype(bf16)
        here = jnp.broadcast_to(high[q : q + 1, :], (8, 128)) == sub_f
        slot = jnp.concatenate([jnp.where(here, float(q), 0.0), jnp.where(here, lane_f, 0.0)], axis=0)
        found += dot1(slot.astype(bf16), onehot)
    row_at, lane_at = found[:8].astype(jnp.int32), found[8:].astype(jnp.int32)

    ring_relay(rad_of, rad_sem)

    wait_all(hr, halo_sem.at[1])

    for f in range(F):
        for t in range(LT):
            side, at = pl.ds(t * 8, 8), pl.ds((f * LT + t) * 8, 8)
            ht[0, at, :] = pltpu.roll(hr[0, side, :], (126 - 2 * f) % 128, 1)
            ht[1, at, :] = pltpu.roll(hr[1, side, :], (128 - 2 * f) % 128, 1) if f else hr[1, side, :]

    def hyper(f, _):
        for t in range(LT):
            base = pl.multiple_of((f * LT + t) * (C * 8), C * 8)
            side = pl.ds(pl.multiple_of((f * LT + t) * 8, 8), 8)
            tiles = [ht[0, side, :]] + [fb[pl.ds(base + c * 8, 8), :] for c in range(C)] + [ht[1, side, :]]
            r1 = [pltpu.roll(v, 1, 1) for v in tiles[:-1]]
            r2 = [pltpu.roll(v, 2, 1) for v in tiles[:-1]]
            m1 = [pltpu.roll(v, 127, 1) for v in tiles[1:]]
            m2 = [pltpu.roll(v, 126, 1) for v in tiles[1:]]
            for c in range(C):
                near = jnp.where(lane < 1, r1[c], r1[c + 1]) + jnp.where(lane >= 127, m1[c + 1], m1[c])
                far = jnp.where(lane < 2, r2[c], r2[c + 1]) + jnp.where(lane >= 126, m2[c + 1], m2[c])
                own = tiles[c + 1]
                fourth = (far - 4.0 * near) + 6.0 * own
                nb[pl.ds(base + c * 8, 8), :] = -NU_HYPER * fourth - own
        return 0

    lax.fori_loop(0, F, hyper, 0, unroll=5)

    wait_all(next_if, near_sem.at[1])
    for f in range(F):
        ifb[l, f] = next_if[f] - lows[f]
    ifb[l, F] = next_if[F] + lows[F]
    ifb[l, F + 1] = v_b
    for d in (2, 1, 3):
        send(ifb.at[l], ifb.at[l], if_sem.at[0], if_sem.at[1], lev_peer(d))

    wait_all(zb.at[pl.ds(1, NZC - 1)], z_sem.at[1])
    lane2 = lax.broadcasted_iota(jnp.int32, (2, 128), 1)
    mine = (lane2 & 31) >> 1 == zc
    packed = jnp.where(mine, code[...], 0.0)
    for d in range(1, NZC):
        source = (zc + NZC - d) % NZC
        packed += pltpu.roll(jnp.where(mine, zb[d], 0.0), (2 * (source - zc) + 128) % 128, 1)
    for h in range(2):
        rows2[h] = packed[h : h + 1, :]
    for dl, dy in plane:
        send(rows2.at[((y + dy) % NY) // 4], ab.at[dl * NY + dy], a_sem.at[0], a_sem.at[1], plane_peer(dl, dy))

    wait_all(rb.at[pl.ds(0, 4 * LB), :], rad_sem.at[3])
    own_out = wot[pl.ds(pl.multiple_of(l * LB, LB), LB), :]

    def network(q, _):
        cols = pl.ds(pl.multiple_of(q * 256, 256), 256)
        hidden = jnp.tanh(jnp.dot(wit[...], rb[:, cols], preferred_element_type=f32)).astype(bf16)
        heat = jnp.dot(own_out, hidden, preferred_element_type=f32)
        for t in range(LT):
            for c in range(2):
                at = pl.multiple_of((t * C + 2 * q + c) * 8, 8)
                hb[pl.ds(at, 8), :] = heat[t * 8 : t * 8 + 8, c * 128 : c * 128 + 128]
        return 0

    lax.fori_loop(0, COLS // 256, network, 0, unroll=4)

    ga = g_b = ka_prev = kb_prev = zero
    for j in range(HALF):
        a, b = j, LB - 1 - j
        ga = (hb[at_level(0, a), :] + ka_prev * ga) * rk[a]
        g_b = (hb[at_level(0, b), :] + kb_prev * g_b) * rk[b]
        hy[a], hy[b] = ga, g_b
        ka_prev, kb_prev = kb[at_level(0, a), :], kb[at_level(0, b - 1), :]
    xa, x_b = middle(ga, g_b)
    hy[HALF - 1], hy[HALF] = xa, x_b
    for j in range(HALF - 2, -1, -1):
        a, b = j, LB - 1 - j
        xa, x_b = hy[a] + rt[a] * xa, hy[b] + rt[b] * x_b
        hy[a], hy[b] = xa, x_b
    hib[l, 0] = xa
    hib[l, 1] = x_b

    for d in (1, 3, 2):
        send(hib.at[l], hib.at[l], hi_sem.at[0], hi_sem.at[1], lev_peer(d))


    wait_all(ifb.at[pl.ds(0, NL - 1)], if_sem.at[1])
    c1, c2 = ifb[1, F + 1], ifb[2, F + 1]
    w0 = 1.0 / ifb[0, F]
    a1 = c1 * w0
    w1 = 1.0 / (ifb[1, F] - c1 * a1)
    a2 = c2 * w1
    w2 = 1.0 / (ifb[2, F] - c2 * a2)

    def fluxes(rise):
        t0 = rise(0)
        t1 = rise(1) + a1 * t0
        t2 = rise(2) + a2 * t1
        f2 = t2 * w2
        f1 = (t1 + c2 * f2) * w1
        f0 = (t0 + c1 * f1) * w0
        below = jnp.where(l == 0, f0, jnp.where(l == 1, f1, jnp.where(l == 2, f2, 0.0)))
        above = jnp.where(l == 1, f0, jnp.where(l == 2, f1, jnp.where(l == 3, f2, 0.0)))
        return below, above

    def correct(of, f, below, above):
        base = f * (LB * C)
        for i in range(LB):
            x = of(i) + ub[i] * below - vb[i] * above
            xb[pl.ds(base + (i // 8) * (C * 8) + i % 8, 8, stride=8), :] = x
        return pl.ds(pl.multiple_of(base, LB * C), LB * C)

    def field(f, _):
        below, above = fluxes(lambda b: ifb[b, f])
        rows = correct(lambda i: gb[f * LB + i], f, below, above)
        ob[rows, :] = (xb[rows, :] + nb[rows, :]).astype(bf16)
        return 0

    lax.fori_loop(1, F, field, 0)

    below, above = fluxes(lambda b: ifb[b, 0])
    rows = correct(lambda i: gb[i], 0, below, above)
    nb[rows, :] = xb[rows, :] + nb[rows, :]
    wait_all(hib.at[pl.ds(0, NL - 1)], hi_sem.at[1])
    below, above = fluxes(lambda b: hib[b + 1, 0] - hib[b, 1])
    correct(lambda i: hy[i], 0, below, above)

    wait_all(ab.at[pl.ds(1, NL * NY - 1)], a_sem.at[1])
    codes = zero
    for dl in range(NL):
        rows = zero
        for dy in range(NY):
            row = ab[dl * NY + dy] if dl or dy else rows2[y // 4]
            rows = jnp.where(sub == (y + NY - dy) % NY, jnp.broadcast_to(row, (8, 128)), rows)
        p = (l + NL - dl) % NL
        moved = pltpu.roll(rows, (32 * (p - y % 4) + 128) % 128, 1)
        codes = jnp.where(lane // 32 == p, moved, codes)
    placed = zero
    for q in range(C):
        row = jnp.broadcast_to(codes[q : q + 1, :], (8, 128))
        placed = jnp.where(row_at == q, jnp.take_along_axis(row, lane_at, axis=1), placed)
    factor = jnp.where(placed > 1.5, 1.0 - f32(CLOUD_SHADE), jnp.where(placed > 0.5, 1.0, 0.0))
    spread = jnp.concatenate([jnp.broadcast_to(factor[c : c + 1, :], (8, 128)) for c in range(C)], axis=0)
    for t in range(LT):
        rows = pl.ds(t * C * 8, C * 8)
        ob[rows, :] = (nb[rows, :] + spread * xb[rows, :]).astype(bf16)

    wait_all(zb.at[pl.ds(1, NZC - 1)], z_sem.at[0])
    wait_all(ab.at[pl.ds(1, NL * NY - 1)], a_sem.at[0])
    wait_all(rb.at[pl.ds(0, 6 * LB), :], rad_sem.at[0])
    wait_all(hs, halo_sem.at[0])
    wait_all(next_if, near_sem.at[0])
    wait_all(ifb.at[pl.ds(0, 3)], if_sem.at[0])
    wait_all(hib.at[pl.ds(0, NL - 1)], hi_sem.at[0])


def tiled(array):
    return array.reshape(-1, 8, C, 128).transpose(0, 2, 1, 3).reshape(-1, 128)


def body(fields, coupling, column_map, sunlit, cloudy, radiation_in, radiation_out):
    f32, bf16 = jnp.float32, jnp.bfloat16
    anywhere = pl.BlockSpec(memory_space=pl.ANY)
    dma = pltpu.SemaphoreType.DMA
    out = pl.pallas_call(
        kernel,
        out_shape=pltpu.VMEM((ROWS, 128), bf16),
        in_specs=[anywhere] * 7,
        out_specs=pl.BlockSpec(memory_space=pltpu.VMEM),
        scratch_shapes=[
            pltpu.VMEM((ROWS, 128), f32),
            pltpu.VMEM((C * LB, 128), f32),
            pltpu.VMEM((8, 128), jnp.int32),
            pltpu.SMEM((2,), jnp.int32),
            pltpu.VMEM((2, 128), jnp.int32),
            pltpu.VMEM((256, 256), bf16),
            pltpu.VMEM((256, 128), bf16),
            pltpu.VMEM((256, 256), bf16),
            pltpu.VMEM((128, 256), bf16),
            pltpu.VMEM((256, COLS), bf16),
            pltpu.VMEM((2, LB, 128), f32),
            pltpu.VMEM((2, LB, 128), f32),
            pltpu.VMEM((2, F * LB, 128), f32),
            pltpu.VMEM((2, 128), f32),
            pltpu.VMEM((2, 1, 128), f32),
            pltpu.VMEM((NL * NY, 1, 128), f32),
            pltpu.VMEM((NZC, 2, 128), f32),
            pltpu.VMEM((F * LB, 8, 128), f32),
            pltpu.VMEM((LB, 8, 128), f32),
            pltpu.VMEM((LB, 8, 128), f32),
            pltpu.VMEM((LB, 8, 128), f32),
            pltpu.VMEM((LB, 8, 128), f32),
            pltpu.VMEM((F + 1, 8, 128), f32),
            pltpu.VMEM((F + 1, 8, 128), f32),
            pltpu.VMEM((F + 1, 8, 128), f32),
            pltpu.VMEM((NL, NIF, 8, 128), f32),
            pltpu.VMEM((NL, 2, 8, 128), f32),
            pltpu.VMEM((LB * C, 128), f32),
            pltpu.VMEM((LB, 8, 128), f32),
            pltpu.VMEM((ROWS, 128), f32),
            pltpu.VMEM((ROWS, 128), f32),
            dma((6,)), dma((2,)), dma((2,)), dma((4,)), dma((2,)), dma((2,)), dma((2,)), dma((2,)),
        ],
        compiler_params=pltpu.CompilerParams(collective_id=0, has_side_effects=True),
        name="column_step",
    )(
        tiled(fields), tiled(coupling), column_map.reshape(8, 128), sunlit,
        cloudy.reshape(2, 128), radiation_in, radiation_out,
    )
    return out.reshape(F * LT, C, 8, 128).transpose(0, 2, 1, 3).reshape(F, LB, COLS)


def solution(mesh):
    placed = (
        P(None, "lev", "elem"),
        P("lev", "elem"),
        P("elem"),
        P(("elem", "lev")),
        P(("elem", "lev")),
        P(),
        P(),
    )
    return jax.shard_map(
        body, mesh=mesh, in_specs=placed, out_specs=P(None, "lev", "elem"), check_vma=False
    )
```

```python
import functools

import jax
import jax.numpy as jnp
from jax import lax
from jax.experimental import pallas as pl
from jax.experimental.pallas import tpu as pltpu
from jax.sharding import PartitionSpec as P

NU_HYPER = 0.05
CLOUD_SHADE = 0.6
MESH = pl.DeviceIdType.MESH

F = 10
NL = 4
NY = 8
NZC = 16
NE = NY * NZC
LB = 32
LT = LB // 8
HALF = LB // 2
COLS = 1024
C = COLS // 128
ROWS = F * LB * C
NIF = F + 2


def dot0(a, b):
    return lax.dot_general(a, b, (((0,), (0,)), ((), ())), preferred_element_type=jnp.float32)


def dot1(a, b):
    return lax.dot_general(a, b, (((1,), (1,)), ((), ())), preferred_element_type=jnp.float32)


def kernel(
    f_hbm, k_hbm, cm_hbm, sun_hbm, cl_hbm, wi_hbm, wo_hbm, ob,
    fb, kb, cm, sun, cl, wi, wo, wit, wot, rb, hs, hr, ht, code, rows2, ab, zb,
    gb, rk, rt, ub, vb, mine_if, next_if, lows, ifb, hib, hb, hy, xb, nb,
    load_sem, a_sem, z_sem, rad_sem, halo_sem, near_sem, if_sem, hi_sem,
):
    f32, bf16 = jnp.float32, jnp.bfloat16
    e = lax.axis_index("elem")
    l = lax.axis_index("lev")
    y, zc = e // NZC, e % NZC

    def lev_peer(d):
        return (e, (l + d) % NL)

    def plane_peer(dl, dy):
        return (((y + dy) % NY) * NZC + zc, (l + dl) % NL)

    def z_peer(d):
        return (y * NZC + (zc + d) % NZC, l)

    right, left = ((e + 1) % NE, l), ((e + NE - 1) % NE, l)
    plane = [(dl, dy) for dy in (4, 3, 5, 2, 6, 1, 7, 0) for dl in (2, 1, 3, 0) if dl or dy]

    def load(src, dst, i):
        copy = pltpu.make_async_copy(src, dst, load_sem.at[i])
        copy.start()
        return copy

    def wait_all(ref, sem):
        pltpu.make_async_copy(ref, ref, sem).wait()

    flags_in = [load(cl_hbm, cl, 0), load(sun_hbm, sun, 1)]

    barrier = pltpu.get_barrier_semaphore()
    peers = [plane_peer(*d) for d in plane] + [z_peer(d) for d in range(1, NZC)] + [right, left]
    for peer in peers:
        pl.semaphore_signal(barrier, inc=1, device_id=peer, device_id_type=MESH)

    n_head = 2 * LB * C
    head = load(f_hbm.at[pl.ds(0, n_head), :], fb.at[pl.ds(0, n_head), :], 2)
    tail = load(f_hbm.at[pl.ds(n_head, ROWS - n_head), :], fb.at[pl.ds(n_head, ROWS - n_head), :], 3)
    k_in = load(k_hbm, kb, 4)
    load(cm_hbm, cm, 5)
    load(wo_hbm, wo, 5)
    for q in range(NL):
        for f in range(2):
            load(wi_hbm.at[pl.ds(f * 128 + q * LB, LB), :], wi.at[pl.ds((q * 2 + f) * LB, LB), :], 5)

    def send(src, dst, ssem, rsem, peer):
        copy = pltpu.make_async_remote_copy(
            src_ref=src, dst_ref=dst, send_sem=ssem, recv_sem=rsem, device_id=peer, device_id_type=MESH
        )
        copy.start()
        return copy

    for copy in flags_in:
        copy.wait()
    for h in range(2):
        code[pl.ds(h, 1), :] = sun[h].astype(f32) * (1.0 + cl[pl.ds(h, 1), :].astype(f32))

    def ring_halves(ref_of, sem):
        for i, (d, h) in enumerate(((1, 0), (NL - 1, 1), (1, 1), (NL - 1, 0))):
            own = ref_of(l, h)
            send(own, own, sem.at[0], sem.at[min(i + 1, 3)], lev_peer(d))

    def ring_relay(ref_of, sem):
        for i, (d, h) in enumerate(((1, 0), (NL - 1, 1))):
            ref = ref_of((l + NL - d) % NL, h)
            wait_all(ref, sem.at[1 + i])
            send(ref, ref, sem.at[0], sem.at[3], lev_peer(d))

    def rad_of(q, h):
        return rb.at[pl.ds(pl.multiple_of((q * 2 + h) * LB, LB), LB), :]

    pl.semaphore_wait(barrier, len(peers))

    for d in range(1, NZC):
        send(code, zb.at[d], z_sem.at[0], z_sem.at[1], z_peer(d))

    own_rad = pl.multiple_of(l * 2 * LB, 2 * LB)
    head.wait()
    for f in range(2):
        for t in range(0, LT, 2):
            for c in range(C):
                at = [((f * LT + t + i) * C + c) * 8 for i in range(2)]
                pair = jnp.concatenate([fb[pl.ds(a, 8), :] for a in at], axis=0)
                rb[pl.ds(own_rad + f * LB + t * 8, 16), pl.ds(c * 128, 128)] = pair.astype(bf16)

    sub = lax.broadcasted_iota(jnp.int32, (8, 128), 0)
    lane = lax.broadcasted_iota(jnp.int32, (8, 128), 1)

    tail.wait()
    for t in range(LT):
        lo_side = hi_side = jnp.zeros((8, 128), f32)
        for f in range(F):
            keep = (lane >= 2 * f) & (lane < 2 * f + 2)
            first = fb[pl.ds((f * LT + t) * C * 8, 8), :]
            last = fb[pl.ds(((f * LT + t) * C + C - 1) * 8, 8), :]
            lo_side = jnp.where(keep, pltpu.roll(first, 2 * f, 1) if f else first, lo_side)
            hi_side = jnp.where(keep, pltpu.roll(last, 2 * f + 2, 1), hi_side)
        hs[0, pl.ds(t * 8, 8), :] = hi_side
        hs[1, pl.ds(t * 8, 8), :] = lo_side
    ring_halves(rad_of, rad_sem)
    send(hs.at[0], hr.at[0], halo_sem.at[0], halo_sem.at[1], right)
    send(hs.at[1], hr.at[1], halo_sem.at[0], halo_sem.at[1], left)

    zero = jnp.zeros((8, 128), f32)

    def at_level(f, i):
        return pl.ds((f * LT + i // 8) * C * 8 + i % 8, 8, stride=8)

    k_in.wait()

    def inward(j, carry):
        ka_prev, kb_prev, sa, sb, gv, gu, gas, gbs = carry
        a, b = j, LB - 1 - j
        ka, kb_ = kb[at_level(0, a), :], kb[at_level(0, b - 1), :]
        da, db = 1.0 + ka_prev * sa, 1.0 + kb_prev * sb
        ra, r_b = 1.0 / (da + ka), 1.0 / (db + kb_)
        rk[a], rk[b] = ra, r_b
        rt[a], rt[b] = ka * ra, kb_ * r_b
        start = jnp.where(j == 0, 1.0, 0.0)
        gv = (start + ka_prev * gv) * ra
        gu = (start + kb_prev * gu) * r_b
        vb[a], ub[b] = gv, gu
        new_a, new_b = [], []
        for f in range(F):
            ga = (fb[at_level(f, a), :] + ka_prev * gas[f]) * ra
            g_b = (fb[at_level(f, b), :] + kb_prev * gbs[f]) * r_b
            gb[f * LB + a], gb[f * LB + b] = ga, g_b
            new_a.append(ga)
            new_b.append(g_b)
        return ka, kb_, da * ra, db * r_b, gv, gu, tuple(new_a), tuple(new_b)

    carry = (zero,) * 6 + ((zero,) * F, (zero,) * F)
    for j in range(HALF):
        carry = inward(j, carry)
    _, _, sa, sb, gv, gu, gas, gbs = carry
    up_mid, down_mid = rt[HALF - 1], rt[HALF]
    mid = 1.0 / (sa + sb * up_mid)

    def middle(ga, g_b):
        xa = (ga + up_mid * g_b) * mid
        return xa, g_b + down_mid * xa

    va, v_b = middle(gv, zero)
    ua, u_b = middle(zero, gu)
    vb[HALF - 1], vb[HALF], ub[HALF - 1], ub[HALF] = va, v_b, ua, u_b
    xas, xbs = [], []
    for f in range(F):
        xa, x_b = middle(gas[f], gbs[f])
        gb[f * LB + HALF - 1], gb[f * LB + HALF] = xa, x_b
        xas.append(xa)
        xbs.append(x_b)
    for j in range(HALF - 2, -1, -1):
        a, b = j, LB - 1 - j
        ratio_a, ratio_b = rt[a], rt[b]
        va, v_b = vb[a] + ratio_a * va, ratio_b * v_b
        ua, u_b = ratio_a * ua, ub[b] + ratio_b * u_b
        vb[a], vb[b], ub[a], ub[b] = va, v_b, ua, u_b
        for f in range(F):
            xas[f] = gb[f * LB + a] + ratio_a * xas[f]
            xbs[f] = gb[f * LB + b] + ratio_b * xbs[f]
            gb[f * LB + a], gb[f * LB + b] = xas[f], xbs[f]
    for f in range(F):
        mine_if[f] = xas[f]
        lows[f] = xbs[f]
    mine_if[F] = va
    lows[F] = u_b + 1.0 / kb[at_level(0, LB - 1), :]
    send(mine_if, next_if, near_sem.at[0], near_sem.at[1], lev_peer(NL - 1))

    wait_all(fb.at[pl.ds(0, 8 + 128 + 256), :], load_sem.at[5])
    wit[...] = wi[...].T
    wot[...] = wo[...].T
    row_i = lax.broadcasted_iota(jnp.int32, (128, 128), 0)
    lane_i = lax.broadcasted_iota(jnp.int32, (128, 128), 1)
    wanted = ((lane_i & 31) >> 1) * 8 + (lane_i >> 5) * 2 + (lane_i & 1)
    order = jnp.where(row_i == wanted, 1.0, 0.0).astype(bf16)
    slots = cm[...]
    parts = jnp.concatenate([slots >> 7, slots & 127], axis=0).astype(f32).astype(bf16)
    parts = jnp.dot(parts, order, preferred_element_type=f32)
    high, low = parts[:8], parts[8:]
    row_f = row_i.astype(f32)
    sub_f, lane_f = sub.astype(f32), lane.astype(f32)
    found = jnp.zeros((16, 128), f32)
    for q in range(C):
        hit = jnp.broadcast_to(low[q : q + 1, :], (128, 128)) == row_f
        onehot = jnp.where(hit, 1.0, 0.0).astype(bf16)
        here = jnp.broadcast_to(high[q : q + 1, :], (8, 128)) == sub_f
        slot = jnp.concatenate([jnp.where(here, float(q), 0.0), jnp.where(here, lane_f, 0.0)], axis=0)
        found += dot1(slot.astype(bf16), onehot)
    row_at, lane_at = found[:8].astype(jnp.int32), found[8:].astype(jnp.int32)

    ring_relay(rad_of, rad_sem)

    wait_all(hr, halo_sem.at[1])

    for f in range(F):
        for t in range(LT):
            side, at = pl.ds(t * 8, 8), pl.ds((f * LT + t) * 8, 8)
            ht[0, at, :] = pltpu.roll(hr[0, side, :], (126 - 2 * f) % 128, 1)
            ht[1, at, :] = pltpu.roll(hr[1, side, :], (128 - 2 * f) % 128, 1) if f else hr[1, side, :]

    def hyper(f, _):
        for t in range(LT):
            base = pl.multiple_of((f * LT + t) * (C * 8), C * 8)
            side = pl.ds(pl.multiple_of((f * LT + t) * 8, 8), 8)
            tiles = [ht[0, side, :]] + [fb[pl.ds(base + c * 8, 8), :] for c in range(C)] + [ht[1, side, :]]
            r1 = [pltpu.roll(v, 1, 1) for v in tiles[:-1]]
            r2 = [pltpu.roll(v, 2, 1) for v in tiles[:-1]]
            m1 = [pltpu.roll(v, 127, 1) for v in tiles[1:]]
            m2 = [pltpu.roll(v, 126, 1) for v in tiles[1:]]
            for c in range(C):
                near = jnp.where(lane < 1, r1[c], r1[c + 1]) + jnp.where(lane >= 127, m1[c + 1], m1[c])
                far = jnp.where(lane < 2, r2[c], r2[c + 1]) + jnp.where(lane >= 126, m2[c + 1], m2[c])
                own = tiles[c + 1]
                fourth = (far - 4.0 * near) + 6.0 * own
                nb[pl.ds(base + c * 8, 8), :] = -NU_HYPER * fourth - own
        return 0

    lax.fori_loop(0, F, hyper, 0, unroll=5)

    wait_all(next_if, near_sem.at[1])
    for f in range(F):
        ifb[l, f] = next_if[f] - lows[f]
    ifb[l, F] = next_if[F] + lows[F]
    ifb[l, F + 1] = v_b
    for d in (2, 1, 3):
        send(ifb.at[l], ifb.at[l], if_sem.at[0], if_sem.at[1], lev_peer(d))

    wait_all(zb.at[pl.ds(1, NZC - 1)], z_sem.at[1])
    lane2 = lax.broadcasted_iota(jnp.int32, (2, 128), 1)
    mine = (lane2 & 31) >> 1 == zc
    packed = jnp.where(mine, code[...], 0.0)
    for d in range(1, NZC):
        source = (zc + NZC - d) % NZC
        packed += pltpu.roll(jnp.where(mine, zb[d], 0.0), (2 * (source - zc) + 128) % 128, 1)
    for h in range(2):
        rows2[h] = packed[h : h + 1, :]
    for dl, dy in plane:
        send(rows2.at[((y + dy) % NY) // 4], ab.at[dl * NY + dy], a_sem.at[0], a_sem.at[1], plane_peer(dl, dy))

    wait_all(rb.at[pl.ds(0, 4 * LB), :], rad_sem.at[3])
    own_out = wot[pl.ds(pl.multiple_of(l * LB, LB), LB), :]

    def network(q, _):
        cols = pl.ds(pl.multiple_of(q * 256, 256), 256)
        hidden = jnp.tanh(jnp.dot(wit[...], rb[:, cols], preferred_element_type=f32)).astype(bf16)
        heat = jnp.dot(own_out, hidden, preferred_element_type=f32)
        for t in range(LT):
            for c in range(2):
                at = pl.multiple_of((t * C + 2 * q + c) * 8, 8)
                hb[pl.ds(at, 8), :] = heat[t * 8 : t * 8 + 8, c * 128 : c * 128 + 128]
        return 0

    lax.fori_loop(0, COLS // 256, network, 0, unroll=4)

    ga = g_b = ka_prev = kb_prev = zero
    for j in range(HALF):
        a, b = j, LB - 1 - j
        ga = (hb[at_level(0, a), :] + ka_prev * ga) * rk[a]
        g_b = (hb[at_level(0, b), :] + kb_prev * g_b) * rk[b]
        hy[a], hy[b] = ga, g_b
        ka_prev, kb_prev = kb[at_level(0, a), :], kb[at_level(0, b - 1), :]
    xa, x_b = middle(ga, g_b)
    hy[HALF - 1], hy[HALF] = xa, x_b
    for j in range(HALF - 2, -1, -1):
        a, b = j, LB - 1 - j
        xa, x_b = hy[a] + rt[a] * xa, hy[b] + rt[b] * x_b
        hy[a], hy[b] = xa, x_b
    hib[l, 0] = xa
    hib[l, 1] = x_b

    for d in (1, 3, 2):
        send(hib.at[l], hib.at[l], hi_sem.at[0], hi_sem.at[1], lev_peer(d))


    wait_all(ifb.at[pl.ds(0, NL - 1)], if_sem.at[1])
    c1, c2 = ifb[1, F + 1], ifb[2, F + 1]
    w0 = 1.0 / ifb[0, F]
    a1 = c1 * w0
    w1 = 1.0 / (ifb[1, F] - c1 * a1)
    a2 = c2 * w1
    w2 = 1.0 / (ifb[2, F] - c2 * a2)

    def fluxes(rise):
        t0 = rise(0)
        t1 = rise(1) + a1 * t0
        t2 = rise(2) + a2 * t1
        f2 = t2 * w2
        f1 = (t1 + c2 * f2) * w1
        f0 = (t0 + c1 * f1) * w0
        below = jnp.where(l == 0, f0, jnp.where(l == 1, f1, jnp.where(l == 2, f2, 0.0)))
        above = jnp.where(l == 1, f0, jnp.where(l == 2, f1, jnp.where(l == 3, f2, 0.0)))
        return below, above

    def correct(of, f, below, above):
        base = f * (LB * C)
        for i in range(LB):
            x = of(i) + ub[i] * below - vb[i] * above
            xb[pl.ds(base + (i // 8) * (C * 8) + i % 8, 8, stride=8), :] = x
        return pl.ds(pl.multiple_of(base, LB * C), LB * C)

    def field(f, _):
        below, above = fluxes(lambda b: ifb[b, f])
        rows = correct(lambda i: gb[f * LB + i], f, below, above)
        ob[rows, :] = (xb[rows, :] + nb[rows, :]).astype(bf16)
        return 0

    lax.fori_loop(1, F, field, 0)

    below, above = fluxes(lambda b: ifb[b, 0])
    rows = correct(lambda i: gb[i], 0, below, above)
    nb[rows, :] = xb[rows, :] + nb[rows, :]
    wait_all(hib.at[pl.ds(0, NL - 1)], hi_sem.at[1])
    below, above = fluxes(lambda b: hib[b + 1, 0] - hib[b, 1])
    correct(lambda i: hy[i], 0, below, above)

    wait_all(ab.at[pl.ds(1, NL * NY - 1)], a_sem.at[1])
    codes = zero
    for dl in range(NL):
        rows = zero
        for dy in range(NY):
            row = ab[dl * NY + dy] if dl or dy else rows2[y // 4]
            rows = jnp.where(sub == (y + NY - dy) % NY, jnp.broadcast_to(row, (8, 128)), rows)
        p = (l + NL - dl) % NL
        moved = pltpu.roll(rows, (32 * (p - y % 4) + 128) % 128, 1)
        codes = jnp.where(lane // 32 == p, moved, codes)
    placed = zero
    for q in range(C):
        row = jnp.broadcast_to(codes[q : q + 1, :], (8, 128))
        placed = jnp.where(row_at == q, jnp.take_along_axis(row, lane_at, axis=1), placed)
    factor = jnp.where(placed > 1.5, 1.0 - f32(CLOUD_SHADE), jnp.where(placed > 0.5, 1.0, 0.0))
    spread = jnp.concatenate([jnp.broadcast_to(factor[c : c + 1, :], (8, 128)) for c in range(C)], axis=0)
    for t in range(LT):
        rows = pl.ds(t * C * 8, C * 8)
        ob[rows, :] = (nb[rows, :] + spread * xb[rows, :]).astype(bf16)

    wait_all(zb.at[pl.ds(1, NZC - 1)], z_sem.at[0])
    wait_all(ab.at[pl.ds(1, NL * NY - 1)], a_sem.at[0])
    wait_all(rb.at[pl.ds(0, 6 * LB), :], rad_sem.at[0])
    wait_all(hs, halo_sem.at[0])
    wait_all(next_if, near_sem.at[0])
    wait_all(ifb.at[pl.ds(0, 3)], if_sem.at[0])
    wait_all(hib.at[pl.ds(0, NL - 1)], hi_sem.at[0])


def tiled(array):
    return array.reshape(-1, 8, C, 128).transpose(0, 2, 1, 3).reshape(-1, 128)


def body(fields, coupling, column_map, sunlit, cloudy, radiation_in, radiation_out):
    f32, bf16 = jnp.float32, jnp.bfloat16
    anywhere = pl.BlockSpec(memory_space=pl.ANY)
    dma = pltpu.SemaphoreType.DMA
    out = pl.pallas_call(
        kernel,
        out_shape=pltpu.VMEM((ROWS, 128), bf16),
        in_specs=[anywhere] * 7,
        out_specs=pl.BlockSpec(memory_space=pltpu.VMEM),
        scratch_shapes=[
            pltpu.VMEM((ROWS, 128), f32),
            pltpu.VMEM((C * LB, 128), f32),
            pltpu.VMEM((8, 128), jnp.int32),
            pltpu.SMEM((2,), jnp.int32),
            pltpu.VMEM((2, 128), jnp.int32),
            pltpu.VMEM((256, 256), bf16),
            pltpu.VMEM((256, 128), bf16),
            pltpu.VMEM((256, 256), bf16),
            pltpu.VMEM((128, 256), bf16),
            pltpu.VMEM((256, COLS), bf16),
            pltpu.VMEM((2, LB, 128), f32),
            pltpu.VMEM((2, LB, 128), f32),
            pltpu.VMEM((2, F * LB, 128), f32),
            pltpu.VMEM((2, 128), f32),
            pltpu.VMEM((2, 1, 128), f32),
            pltpu.VMEM((NL * NY, 1, 128), f32),
            pltpu.VMEM((NZC, 2, 128), f32),
            pltpu.VMEM((F * LB, 8, 128), f32),
            pltpu.VMEM((LB, 8, 128), f32),
            pltpu.VMEM((LB, 8, 128), f32),
            pltpu.VMEM((LB, 8, 128), f32),
            pltpu.VMEM((LB, 8, 128), f32),
            pltpu.VMEM((F + 1, 8, 128), f32),
            pltpu.VMEM((F + 1, 8, 128), f32),
            pltpu.VMEM((F + 1, 8, 128), f32),
            pltpu.VMEM((NL, NIF, 8, 128), f32),
            pltpu.VMEM((NL, 2, 8, 128), f32),
            pltpu.VMEM((LB * C, 128), f32),
            pltpu.VMEM((LB, 8, 128), f32),
            pltpu.VMEM((ROWS, 128), f32),
            pltpu.VMEM((ROWS, 128), f32),
            dma((6,)), dma((2,)), dma((2,)), dma((4,)), dma((2,)), dma((2,)), dma((2,)), dma((2,)),
        ],
        compiler_params=pltpu.CompilerParams(collective_id=0, has_side_effects=True),
        name="column_step",
    )(
        tiled(fields), tiled(coupling), column_map.reshape(8, 128), sunlit,
        cloudy.reshape(2, 128), radiation_in, radiation_out,
    )
    return out.reshape(F * LT, C, 8, 128).transpose(0, 2, 1, 3).reshape(F, LB, COLS)


def solution(mesh):
    placed = (
        P(None, "lev", "elem"),
        P("lev", "elem"),
        P("elem"),
        P(("elem", "lev")),
        P(("elem", "lev")),
        P(),
        P(),
    )
    return jax.shard_map(
        body, mesh=mesh, in_specs=placed, out_specs=P(None, "lev", "elem"), check_vma=False
    )
```
